32 devices in a mesh: row: 4 (over z), col: 8 (over y, x, core).
Axes of the slice: x: 2, y: 2, z: 4, core: 2. Of those that a mesh axis runs over, the one named last changes fastest.
Arguments:
- tokens: bfloat16 [512, 8192], P('col', 'row'), may hold values from -6 to 6
- w_gate: bfloat16 [8192, 16384], P('row', 'col'), may hold values from -0.09375 to 0.09375
- w_up: bfloat16 [8192, 16384], P('row', 'col'), may hold values from -0.09375 to 0.09375
- w_down: bfloat16 [16384, 8192], P('col', 'row'), may hold values from -0.0625 to 0.0625
- mask_in: int32 [64, 32], P('col', 'row'), may hold values 0 or 1
- mask_out: int32 [64, 32], P('col', 'row'), may hold values 0 or 1
- out_grad: bfloat16 [512, 8192], P('col', 'row'), may hold values from -6 to 6
Outputs:
- output: bfloat16 [512, 8192], P('col', 'row')
- tokens_grad: bfloat16 [512, 8192], P('col', 'row')
- gate_wgrad: bfloat16 [8192, 16384], P('row', 'col')
- up_wgrad: bfloat16 [8192, 16384], P('row', 'col')
- down_wgrad: bfloat16 [16384, 8192], P('col', 'row')
The draws below stay inside these ranges and needn't reach their ends.
All inputs are finite; a program needn't handle non-finite values. No bound on the sum of `mask_in` or of `mask_out` on one device may be relied on, other than what follows from the above.
Results may differ from the reference program's by a relative error of at most 0.0049.
Values may be sent and summed in bfloat16 or wider, within the bound.
A program may use at most 128 MiB of HBM per device.

```python
import jax
import jax.numpy as jnp

D = 8192
FF = 16384
BLOCK = 256
TOKENS = 512
FFB = 64
DB = 32


def touch_ends(values, stream_key, smallest, top_value):
    longest = values.shape.index(max(values.shape))
    spots = []
    for shift in (0, 1):
        where = [jax.random.randint(jax.random.fold_in(stream_key, axis), (), 0, length) for axis, length in enumerate(values.shape)]
        where[longest] = (where[longest] + shift) % values.shape[longest]
        spots.append(tuple(where))
    return values.at[spots[0]].set(smallest).at[spots[1]].set(top_value)


def level_of(stream_key, shape, split, smallest, high):
    gain, own = 1.0, jax.random.fold_in(stream_key, 6)
    for axis_at, parts in split:
        draws = jnp.exp(jax.random.uniform(jax.random.fold_in(own, axis_at), (parts,), jnp.float32, smallest / len(split), high / len(split)))
        gain = gain * jnp.repeat(draws, shape[axis_at] // parts).reshape([-1 if axis == axis_at else 1 for axis in range(len(shape))])
    return gain


def centred(rng, shape, scale, most, split=(), held_as=jnp.bfloat16):
    entries = scale * jax.random.normal(rng, shape, jnp.float32)
    if split:
        entries = entries * level_of(rng, shape, split, -0.22, 0.18)
    return jnp.clip(entries, -most, most).astype(held_as)


def setup_inputs(seed: int = 0) -> dict:
    streams_of = jax.random.split(jax.random.key(seed), 8)
    return {
        "tokens": centred(streams_of[0], (TOKENS, D), 1.0, 6.0, ((0, 8), (1, 4))),
        "w_gate": centred(streams_of[1], (D, FF), (D // 2) ** -0.5, 0.09375, ((0, 4), (1, 8))),
        "w_up": centred(streams_of[2], (D, FF), (D // 2) ** -0.5, 0.09375, ((0, 4), (1, 8))),
        "w_down": centred(streams_of[3], (FF, D), (FF // 2) ** -0.5, 0.0625, ((0, 8), (1, 4))),
        "mask_in": touch_ends((jax.random.randint(streams_of[4], (FFB, DB), 0, 2) < 1).astype(jnp.int32), jax.random.fold_in(streams_of[4], 1), 0, 1),
        "mask_out": touch_ends((jax.random.randint(streams_of[5], (FFB, DB), 0, 2) < 1).astype(jnp.int32), jax.random.fold_in(streams_of[5], 1), 0, 1),
        "out_grad": centred(streams_of[6], (TOKENS, D), 1.0, 6.0, ((0, 8), (1, 4))),
    }


def spread(mask_tile):
    return jnp.repeat(jnp.repeat(mask_tile.T, BLOCK, axis=0), BLOCK, axis=1)


def reference(tokens, w_gate, w_up, w_down, mask_in, mask_out, out_grad):
    keep_in = spread(mask_in).astype(jnp.bfloat16)
    keep_out = spread(mask_out).T.astype(jnp.bfloat16)
    gate_masked = w_gate * keep_in
    up_masked = w_up * keep_in
    down_masked = w_down * keep_out
    gate = jnp.dot(tokens, gate_masked, preferred_element_type=jnp.float32)
    up = jnp.dot(tokens, up_masked, preferred_element_type=jnp.float32)
    sigmoid_gate = jax.nn.sigmoid(gate)
    hidden = (gate * sigmoid_gate * up).astype(jnp.bfloat16)
    output = jnp.dot(hidden, down_masked, preferred_element_type=jnp.float32).astype(jnp.bfloat16)
    hidden_grad = jnp.dot(out_grad, down_masked.T, preferred_element_type=jnp.float32)
    up_grad = (hidden_grad * gate * sigmoid_gate).astype(jnp.bfloat16)
    gate_grad = (hidden_grad * up * sigmoid_gate * (1.0 + gate * (1.0 - sigmoid_gate))).astype(jnp.bfloat16)
    down_wgrad = (jnp.dot(hidden.T, out_grad, preferred_element_type=jnp.float32) * keep_out.astype(jnp.float32)).astype(jnp.bfloat16)
    gate_wgrad = (jnp.dot(tokens.T, gate_grad, preferred_element_type=jnp.float32) * keep_in.astype(jnp.float32)).astype(jnp.bfloat16)
    up_wgrad = (jnp.dot(tokens.T, up_grad, preferred_element_type=jnp.float32) * keep_in.astype(jnp.float32)).astype(jnp.bfloat16)
    tokens_grad = (jnp.dot(gate_grad, gate_masked.T, preferred_element_type=jnp.float32)
                   + jnp.dot(up_grad, up_masked.T, preferred_element_type=jnp.float32)).astype(jnp.bfloat16)
    return (output, tokens_grad, gate_wgrad, up_wgrad, down_wgrad)
```

```python
import functools

import jax
import jax.numpy as jnp
from jax import lax
from jax.experimental import pallas as pl
from jax.experimental.pallas import tpu as pltpu
from jax.sharding import PartitionSpec as P

BLOCK = 256
CORES = 2
LAG_OWN = 1
LAG_FWD = 3
LAG_USE = 5
OWN_SLOTS = LAG_OWN + 1
MESH = pl.DeviceIdType.MESH
F32 = jnp.float32
BF16 = jnp.bfloat16


def dot(left, right, dims):
    return lax.dot_general(left, right, (dims, ((), ())), preferred_element_type=F32)


def turned(chunk):
    return chunk % 128 == 0


def flip(chip, j, chips):
    other, bit = chip, 1
    while bit < chips:
        other = other + lax.rem(lax.div(j, bit), 2) * (bit - 2 * bit * lax.rem(lax.div(chip, bit), 2))
        bit *= 2
    return other


def place(q, chips):
    return jnp.where(q == 0, 0, jnp.where(q == chips - 1, 1, q + 1))


def step_kernel(
    rows, cols, units,
    tok, cot, w_gate, w_up, w_down, keep_in, keep_out,
    base, tail, xt_out, dy_out, fin_out, ht_out,
    x, dy, xt, part, other, fin, ht, own, w_in, w_dn, acc, sib, rs_send, rs_recv,
    own_s, sib_ss, sib_rs, ag_ss, ag_rs, fw_ss, fw_rs, w_s, p_ss, a_rs, b_rs, fi_ss, fo_ss, f_rs,
    xt_s, dy_s, fin_s, ht_s, rx_ss, rx_rs, rs_ss, rs_rs, end_s,
):
    r = lax.axis_index("row")
    c = lax.axis_index("col")
    chips = cols // CORES
    chip, core = lax.div(c, CORES), lax.rem(c, CORES)
    low = r < rows // 2
    inner = jnp.where(low, r + 1, r - 1)
    outer = jnp.where(low, r - 1, r + 1)
    has_outer = (r > 0) & (r < rows - 1)
    middle = (r == rows // 2 - 1) | (r == rows // 2)
    owned = jnp.where(low, 0, 1)
    given = 1 - owned
    share, width = tok.shape
    chunk = CORES * share
    half = chunk // 2
    pieces = width // BLOCK
    count = chips * units
    turn = turned(chunk)
    sibling = (r, chip * CORES + (1 - core))

    def partner(q):
        return (r, flip(chip, place(q, chips), chips) * CORES + core)

    def halves(h):
        return pl.ds(pl.multiple_of(h * half, half), half)

    def shares(e):
        return pl.ds(pl.multiple_of(e * share, share), share)

    def blocks(i):
        return pl.ds(pl.multiple_of(i * BLOCK, BLOCK), BLOCK)

    def chunks(q):
        return pl.ds(pl.multiple_of(q * chunk, chunk), chunk)

    def weights(k):
        return (
            pltpu.make_async_copy(w_gate.at[:, blocks(k)], w_in.at[k, 0], w_s.at[k, 0]),
            pltpu.make_async_copy(w_up.at[:, blocks(k)], w_in.at[k, 1], w_s.at[k, 1]),
            pltpu.make_async_copy(w_down.at[blocks(k), :], w_dn.at[k], w_s.at[k, 2]),
        )

    def own_copy(a):
        src, dst = ((tok, x), (cot, dy))[a]
        return pltpu.make_async_copy(src, dst.at[0, shares(core), :], own_s.at[a])

    for a in range(2):
        own_copy(a).start()
    for copy in weights(0):
        copy.start()

    barrier = pltpu.get_barrier_semaphore()
    pl.semaphore_signal(barrier, inc=1, device_id=(inner, c), device_id_type=MESH)
    pl.semaphore_signal(barrier, inc=1, device_id=sibling, device_id_type=MESH)
    for q in range(1, chips):
        pl.semaphore_signal(barrier, inc=1, device_id=partner(q), device_id_type=MESH)

    @pl.when(has_outer)
    def _():
        pl.semaphore_signal(barrier, inc=1, device_id=(outer, c), device_id_type=MESH)

    pl.semaphore_wait(barrier, jnp.where(has_outer, chips + 2, chips + 1))

    def to_sibling(a):
        src, dst = ((tok, x), (cot, dy))[a]
        return pltpu.make_async_remote_copy(
            src_ref=src, dst_ref=dst.at[0, shares(core), :], send_sem=sib_ss.at[a],
            recv_sem=sib_rs.at[a], device_id=sibling, device_id_type=MESH,
        )

    def to_chip(a, q):
        src, dst = ((tok, x), (cot, dy))[a]
        return pltpu.make_async_remote_copy(
            src_ref=src, dst_ref=dst.at[q, shares(core), :], send_sem=ag_ss.at[a, q - 1],
            recv_sem=ag_rs.at[a, q - 1], device_id=partner(q), device_id_type=MESH,
        )

    def forward(a, q):
        ref = (x, dy)[a].at[q, shares(core), :]
        return pltpu.make_async_remote_copy(
            src_ref=ref, dst_ref=ref, send_sem=fw_ss.at[a, q - 1],
            recv_sem=fw_rs.at[a, q - 1], device_id=sibling, device_id_type=MESH,
        )

    for a in range(2):
        to_sibling(a).start()
    for q in range(1, chips):
        for a in range(2):
            to_chip(a, q).start()

    @pl.loop(1, units)
    def _(k):
        for copy in weights(k):
            copy.start()

    def send_inner(t, h):
        ref = part.at[t, :, halves(h), :]
        return pltpu.make_async_remote_copy(
            src_ref=ref, dst_ref=ref, send_sem=p_ss.at[t, h],
            recv_sem=a_rs.at[t, h], device_id=(inner, c), device_id_type=MESH,
        )

    def send_middle(t):
        return pltpu.make_async_remote_copy(
            src_ref=part.at[t, :, halves(given), :], dst_ref=other.at[t], send_sem=p_ss.at[t, given],
            recv_sem=b_rs.at[t], device_id=(inner, c), device_id_type=MESH,
        )

    def share_inner(t, h):
        ref = fin.at[t, :, halves(h), :]
        return pltpu.make_async_remote_copy(
            src_ref=ref, dst_ref=ref, send_sem=fi_ss.at[t],
            recv_sem=f_rs.at[t, h], device_id=(inner, c), device_id_type=MESH,
        )

    def share_outer(t, h):
        ref = fin.at[t, :, halves(h), :]
        return pltpu.make_async_remote_copy(
            src_ref=ref, dst_ref=ref, send_sem=fo_ss.at[t, h],
            recv_sem=f_rs.at[t, h], device_id=(outer, c), device_id_type=MESH,
        )

    def save_xt(q):
        if not turn:
            return pltpu.make_async_copy(x.at[q], xt_out.at[chunks(q), :], xt_s.at[q])
        return pltpu.make_async_copy(xt.at[lax.rem(q, 2)], xt_out.at[:, chunks(q)], xt_s.at[q])

    def save_dy(q):
        return pltpu.make_async_copy(dy.at[q], dy_out.at[chunks(q), :], dy_s.at[q])

    def save_fin(t):
        q, k = lax.div(t, units), lax.rem(t, units)
        return pltpu.make_async_copy(
            fin.at[t, pl.ds(0, 2)], fin_out.at[:, chunks(q), blocks(k)], fin_s.at[t]
        )

    def save_ht(t):
        q, k = lax.div(t, units), lax.rem(t, units)
        if not turn:
            return pltpu.make_async_copy(fin.at[t, 2], ht_out.at[chunks(q), blocks(k)], ht_s.at[t])
        return pltpu.make_async_copy(ht.at[t], ht_out.at[blocks(k), chunks(q)], ht_s.at[t])

    def produce(t):
        q, k = lax.div(t, units), lax.rem(t, units)
        s = lax.rem(t, OWN_SLOTS)

        @pl.when(t == 0)
        def _():
            own_copy(0).wait()
            to_sibling(0).wait_recv()

        @pl.when((k == 0) & (q > 0))
        def _():
            for a in range(2):
                forward(a, q).wait_recv()

        @pl.when(q == 0)
        def _():
            for copy in weights(k):
                copy.wait()

            @pl.loop(0, pieces)
            def _(i):
                at = blocks(i)
                keep = keep_in[k, i].astype(F32)
                w_in[k, 0, at, :] = (w_in[k, 0, at, :].astype(F32) * keep).astype(BF16)
                w_in[k, 1, at, :] = (w_in[k, 1, at, :].astype(F32) * keep).astype(BF16)
                w_dn[k, :, at] = (w_dn[k, :, at].astype(F32) * keep_out[k, i].astype(F32)).astype(BF16)

        own[s, 0] = dot(x[q], w_in[k, 0], ((1,), (0,)))
        own[s, 1] = dot(x[q], w_in[k, 1], ((1,), (0,)))

        @pl.when(t == 0)
        def _():
            own_copy(1).wait()
            to_sibling(1).wait_recv()

        own[s, 2] = dot(dy[q], w_dn[k], ((1,), (1,)))

    def reduce(t):
        s = lax.rem(t, OWN_SLOTS)

        def rounded(h):
            at = halves(h)

            @pl.when(has_outer)
            def _():
                send_inner(t, h).wait_recv()
                for j in range(3):
                    part[t, j, at, :] = (own[s, j, at, :] + part[t, j, at, :].astype(F32)).astype(BF16)

            @pl.when(jnp.logical_not(has_outer))
            def _():
                for j in range(3):
                    part[t, j, at, :] = own[s, j, at, :].astype(BF16)

        rounded(given)

        @pl.when(middle)
        def _():
            send_middle(t).start()

        @pl.when(jnp.logical_not(middle))
        def _():
            send_inner(t, given).start()
            rounded(owned)
            send_inner(t, owned).start()

    def finish(t):
        s = lax.rem(t, OWN_SLOTS)
        at = halves(owned)

        @pl.when(middle)
        def _():
            @pl.when(has_outer)
            def _():
                send_inner(t, owned).wait_recv()
                for j in range(3):
                    own[s, j, at, :] += part[t, j, at, :].astype(F32)

            send_middle(t).wait_recv()
            gate = own[s, 0, at, :] + other[t, 0].astype(F32)
            up = own[s, 1, at, :] + other[t, 1].astype(F32)
            grad = own[s, 2, at, :] + other[t, 2].astype(F32)
            sig = jax.nn.sigmoid(gate)
            act = gate * sig
            fin[t, 0, at, :] = (grad * up * sig * (1.0 + gate * (1.0 - sig))).astype(BF16)
            fin[t, 1, at, :] = (grad * act).astype(BF16)
            fin[t, 2, at, :] = (act * up).astype(BF16)
            share_inner(t, owned).start()

            @pl.when(has_outer)
            def _():
                share_outer(t, owned).start()

    def arrived(t):
        share_inner(t, given).wait_recv()

        @pl.when(has_outer)
        def _():
            share_outer(t, given).start()

        @pl.when(jnp.logical_not(middle))
        def _():
            share_inner(t, owned).wait_recv()

            @pl.when(has_outer)
            def _():
                share_outer(t, owned).start()

    def transpose_tokens(t):
        q, k = lax.div(t, units), lax.rem(t, units)

        if turn:
            @pl.when((k == 0) & (q >= 2))
            def _():
                save_xt(q - 2).wait()

            @pl.loop(lax.div(k * pieces, units), lax.div((k + 1) * pieces, units))
            def _(i):
                xt[lax.rem(q, 2), blocks(i), :] = x[q, :, blocks(i)].T

        @pl.when(k == units - 1)
        def _():
            save_xt(q).start()
            save_dy(q).start()

        @pl.when((k == units // 2) & (q + 1 < chips))
        def _():
            for a in range(2):
                to_chip(a, q + 1).wait_recv()
                forward(a, q + 1).start()

    def to_sibling_sum(q):
        return pltpu.make_async_remote_copy(
            src_ref=acc.at[lax.rem(q, 2), :, shares(1 - core), :], dst_ref=sib.at[q],
            send_sem=rx_ss.at[q], recv_sem=rx_rs.at[q], device_id=sibling, device_id_type=MESH,
        )

    def scatter(q):
        return pltpu.make_async_remote_copy(
            src_ref=rs_send.at[q - 1], dst_ref=rs_recv.at[q - 1], send_sem=rs_ss.at[q - 1],
            recv_sem=rs_rs.at[q - 1], device_id=partner(q), device_id_type=MESH,
        )

    def consume(t):
        q, k = lax.div(t, units), lax.rem(t, units)
        b = lax.rem(q, 2)

        @pl.when(k == 0)
        def _():
            acc[b] = jnp.zeros_like(acc[b])

        save_fin(t).start()
        acc[b, 0] += dot(fin[t, 2], w_dn[k], ((1,), (0,)))
        acc[b, 1] += dot(fin[t, 0], w_in[k, 0], ((1,), (1,))) + dot(
            fin[t, 1], w_in[k, 1], ((1,), (1,))
        )

        @pl.when(k == units - 1)
        def _():
            to_sibling_sum(q).start()

        if turn:
            ht[t] = fin[t, 2].T
        save_ht(t).start()

    def settle(q):
        to_sibling_sum(q).wait()
        at = shares(core)
        for a in range(2):
            sib[q, a] += acc[lax.rem(q, 2), a, at, :]

    @pl.loop(0, count + LAG_USE)
    def _(t):
        @pl.when(t < count)
        def _():
            produce(t)
            reduce(t)

        @pl.when((t >= LAG_OWN) & (t < count + LAG_OWN))
        def _():
            finish(t - LAG_OWN)

        @pl.when(has_outer & (t >= LAG_FWD) & (t < count + LAG_FWD))
        def _():
            arrived(t - LAG_FWD)

        @pl.when(t < count)
        def _():
            transpose_tokens(t)

        @pl.when(t >= LAG_USE)
        def _():
            u = t - LAG_USE

            @pl.when(jnp.logical_not(has_outer))
            def _():
                arrived(u)

            consume(u)
            q = lax.div(u, units) - 1

            @pl.when((lax.rem(u, units) == 1) & (q >= 0))
            def _():
                settle(q)

                @pl.when(q > 0)
                def _():
                    for a in range(2):
                        rs_send[q - 1, a] = sib[q, a].astype(BF16)
                    scatter(q).start()

    last = chips - 1
    for q in range(1, last):
        scatter(q).wait()
        for a in range(2):
            sib[0, a] += rs_recv[q - 1, a].astype(F32)
    save_base = pltpu.make_async_copy(sib.at[0], base, end_s.at[0])
    save_base.start()
    settle(last)
    for a in range(2):
        rs_send[last - 1, a] = sib[last, a].astype(BF16)
    save_tail = pltpu.make_async_copy(rs_send.at[last - 1], tail, end_s.at[1])
    save_tail.start()

    @pl.loop(0, count)
    def _(t):
        save_fin(t).wait()
        save_ht(t).wait()

        @pl.when(middle)
        def _():
            send_middle(t).wait_send()
            share_inner(t, owned).wait_send()

        @pl.when(jnp.logical_not(middle))
        def _():
            for h in range(2):
                send_inner(t, h).wait_send()

        @pl.when(has_outer)
        def _():
            for h in range(2):
                share_outer(t, h).wait_send()

    for a in range(2):
        to_sibling(a).wait_send()
        for q in range(1, chips):
            to_chip(a, q).wait_send()
            forward(a, q).wait_send()
    for q in range(chips):
        save_dy(q).wait()
        if q >= chips - 2 or not turn:
            save_xt(q).wait()
    save_base.wait()
    save_tail.wait()


def wgrad_kernel(xt, dy, fin, ht, keep_in, keep_out, gate_w, up_w, down_w):
    k = pl.program_id(0)
    pieces = xt.shape[0] // BLOCK

    @pl.loop(0, pieces)
    def _(i):
        at = pl.ds(pl.multiple_of(i * BLOCK, BLOCK), BLOCK)

        @pl.when(keep_in[k, i] != 0)
        def _():
            gate_w[at, :] = dot(xt[at, :], fin[0], ((1,), (0,))).astype(BF16)
            up_w[at, :] = dot(xt[at, :], fin[1], ((1,), (0,))).astype(BF16)

        @pl.when(keep_in[k, i] == 0)
        def _():
            gate_w[at, :] = jnp.zeros((BLOCK, BLOCK), BF16)
            up_w[at, :] = jnp.zeros((BLOCK, BLOCK), BF16)

        @pl.when(keep_out[k, i] != 0)
        def _():
            down_w[:, at] = dot(ht[...], dy[:, at], ((1,), (0,))).astype(BF16)

        @pl.when(keep_out[k, i] == 0)
        def _():
            down_w[:, at] = jnp.zeros((BLOCK, BLOCK), BF16)


def local(rows, cols, tokens, w_gate, w_up, w_down, mask_in, mask_out, out_grad):
    share, width = tokens.shape
    hidden = w_gate.shape[1]
    units = hidden // BLOCK
    total = share * cols
    chips = cols // CORES
    chunk = CORES * share
    count = chips * units
    smem = pl.BlockSpec(memory_space=pltpu.SMEM)
    anywhere = pl.BlockSpec(memory_space=pl.ANY)
    dma = pltpu.SemaphoreType.DMA
    struct = jax.ShapeDtypeStruct
    base, tail, xt, dy, fin, ht = pl.pallas_call(
        functools.partial(step_kernel, rows, cols, units),
        out_shape=(
            struct((2, share, width), F32),
            struct((2, share, width), BF16),
            struct((width, total) if turned(chunk) else (total, width), BF16),
            struct((total, width), BF16),
            struct((2, total, hidden), BF16),
            struct((hidden, total) if turned(chunk) else (total, hidden), BF16),
        ),
        in_specs=[anywhere] * 5 + [smem] * 2,
        out_specs=(anywhere,) * 6,
        scratch_shapes=[
            pltpu.VMEM((chips, chunk, width), BF16),
            pltpu.VMEM((chips, chunk, width), BF16),
            pltpu.VMEM((2, width, chunk), BF16),
            pltpu.VMEM((count, 3, chunk, BLOCK), BF16),
            pltpu.VMEM((count, 3, chunk // 2, BLOCK), BF16),
            pltpu.VMEM((count, 3, chunk, BLOCK), BF16),
            pltpu.VMEM((count, BLOCK, chunk) if turned(chunk) else (1, 16, 128), BF16),
            pltpu.VMEM((OWN_SLOTS, 3, chunk, BLOCK), F32),
            pltpu.VMEM((units, 2, width, BLOCK), BF16),
            pltpu.VMEM((units, BLOCK, width), BF16),
            pltpu.VMEM((2, 2, chunk, width), F32),
            pltpu.VMEM((chips, 2, share, width), F32),
            pltpu.VMEM((chips - 1, 2, share, width), BF16),
            pltpu.VMEM((chips - 2, 2, share, width), BF16),
            dma((2,)), dma((2,)), dma((2,)),
            dma((2, chips - 1)), dma((2, chips - 1)),
            dma((2, chips - 1)), dma((2, chips - 1)),
            dma((units, 3)),
            dma((count, 2)), dma((count, 2)), dma((count,)),
            dma((count,)), dma((count, 2)), dma((count, 2)),
            dma((chips,)), dma((chips,)), dma((count,)), dma((count,)),
            dma((chips,)), dma((chips,)),
            dma((chips - 2,)), dma((chips - 2,)),
            dma((2,)),
        ],
        compiler_params=pltpu.CompilerParams(
            collective_id=0, has_side_effects=True, vmem_limit_bytes=63 * 1024 * 1024
        ),
        cost_estimate=pl.CostEstimate(
            flops=12 * total * width * hidden,
            bytes_accessed=6 * width * hidden,
            transcendentals=total * hidden,
        ),
        name="step",
    )(tokens, out_grad, w_gate, w_up, w_down, mask_in, mask_out)
    if not turned(chunk):
        xt, ht = xt.T, ht.T
    nearest = [(i, (i // CORES ^ 1) * CORES + i % CORES) for i in range(cols)]
    moved = lax.ppermute(tail, "col", nearest)
    gate_wgrad, up_wgrad, down_wgrad = pl.pallas_call(
        wgrad_kernel,
        grid=(units,),
        out_shape=(
            struct((width, hidden), BF16),
            struct((width, hidden), BF16),
            struct((hidden, width), BF16),
        ),
        in_specs=[
            pl.BlockSpec((width, total), lambda k: (0, 0)),
            pl.BlockSpec((total, width), lambda k: (0, 0)),
            pl.BlockSpec((2, total, BLOCK), lambda k: (0, 0, k)),
            pl.BlockSpec((BLOCK, total), lambda k: (k, 0)),
            smem,
            smem,
        ],
        out_specs=(
            pl.BlockSpec((width, BLOCK), lambda k: (0, k)),
            pl.BlockSpec((width, BLOCK), lambda k: (0, k)),
            pl.BlockSpec((BLOCK, width), lambda k: (k, 0)),
        ),
        compiler_params=pltpu.CompilerParams(vmem_limit_bytes=60 * 1024 * 1024),
        cost_estimate=pl.CostEstimate(
            flops=6 * total * width * hidden,
            bytes_accessed=6 * width * hidden + 10 * total * width,
            transcendentals=0,
        ),
        name="wgrad",
    )(xt, dy, fin, ht, mask_in, mask_out)
    result = (base + moved.astype(F32)).astype(BF16)
    return result[0], result[1], gate_wgrad, up_wgrad, down_wgrad


def solution(mesh):
    placed = (
        P("col", "row"),
        P("row", "col"),
        P("row", "col"),
        P("col", "row"),
        P("col", "row"),
        P("col", "row"),
        P("col", "row"),
    )
    return jax.shard_map(
        functools.partial(local, mesh.shape["row"], mesh.shape["col"]),
        mesh=mesh,
        in_specs=placed,
        out_specs=(
            P("col", "row"),
            P("col", "row"),
            P("row", "col"),
            P("row", "col"),
            P("col", "row"),
        ),
        check_vma=False,
    )
```

```python
import functools

import jax
import jax.numpy as jnp
from jax import lax
from jax.experimental import pallas as pl
from jax.experimental.pallas import tpu as pltpu
from jax.sharding import PartitionSpec as P

BLOCK = 256
CORES = 2
LAG_OWN = 1
LAG_FWD = 3
LAG_USE = 5
OWN_SLOTS = LAG_OWN + 1
MESH = pl.DeviceIdType.MESH
F32 = jnp.float32
BF16 = jnp.bfloat16


def dot(left, right, dims):
    return lax.dot_general(left, right, (dims, ((), ())), preferred_element_type=F32)


def turned(chunk):
    return chunk % 128 == 0


def flip(chip, j, chips):
    other, bit = chip, 1
    while bit < chips:
        other = other + lax.rem(lax.div(j, bit), 2) * (bit - 2 * bit * lax.rem(lax.div(chip, bit), 2))
        bit *= 2
    return other


def place(q, chips):
    return jnp.where(q == 0, 0, jnp.where(q == chips - 1, 1, q + 1))


def step_kernel(
    rows, cols, units,
    tok, cot, w_gate, w_up, w_down, keep_in, keep_out,
    base, tail, xt_out, dy_out, fin_out, ht_out,
    x, dy, xt, part, other, fin, ht, own, w_in, w_dn, acc, sib, rs_send, rs_recv,
    own_s, sib_ss, sib_rs, ag_ss, ag_rs, fw_ss, fw_rs, w_s, p_ss, a_rs, b_rs, fi_ss, fo_ss, f_rs,
    xt_s, dy_s, fin_s, ht_s, rx_ss, rx_rs, rs_ss, rs_rs, end_s,
):
    r = lax.axis_index("row")
    c = lax.axis_index("col")
    chips = cols // CORES
    chip, core = lax.div(c, CORES), lax.rem(c, CORES)
    low = r < rows // 2
    inner = jnp.where(low, r + 1, r - 1)
    outer = jnp.where(low, r - 1, r + 1)
    has_outer = (r > 0) & (r < rows - 1)
    middle = (r == rows // 2 - 1) | (r == rows // 2)
    owned = jnp.where(low, 0, 1)
    given = 1 - owned
    share, width = tok.shape
    chunk = CORES * share
    half = chunk // 2
    pieces = width // BLOCK
    count = chips * units
    turn = turned(chunk)
    sibling = (r, chip * CORES + (1 - core))

    def partner(q):
        return (r, flip(chip, place(q, chips), chips) * CORES + core)

    def halves(h):
        return pl.ds(pl.multiple_of(h * half, half), half)

    def shares(e):
        return pl.ds(pl.multiple_of(e * share, share), share)

    def blocks(i):
        return pl.ds(pl.multiple_of(i * BLOCK, BLOCK), BLOCK)

    def chunks(q):
        return pl.ds(pl.multiple_of(q * chunk, chunk), chunk)

    def weights(k):
        return (
            pltpu.make_async_copy(w_gate.at[:, blocks(k)], w_in.at[k, 0], w_s.at[k, 0]),
            pltpu.make_async_copy(w_up.at[:, blocks(k)], w_in.at[k, 1], w_s.at[k, 1]),
            pltpu.make_async_copy(w_down.at[blocks(k), :], w_dn.at[k], w_s.at[k, 2]),
        )

    def own_copy(a):
        src, dst = ((tok, x), (cot, dy))[a]
        return pltpu.make_async_copy(src, dst.at[0, shares(core), :], own_s.at[a])

    for a in range(2):
        own_copy(a).start()
    for copy in weights(0):
        copy.start()

    barrier = pltpu.get_barrier_semaphore()
    pl.semaphore_signal(barrier, inc=1, device_id=(inner, c), device_id_type=MESH)
    pl.semaphore_signal(barrier, inc=1, device_id=sibling, device_id_type=MESH)
    for q in range(1, chips):
        pl.semaphore_signal(barrier, inc=1, device_id=partner(q), device_id_type=MESH)

    @pl.when(has_outer)
    def _():
        pl.semaphore_signal(barrier, inc=1, device_id=(outer, c), device_id_type=MESH)

    pl.semaphore_wait(barrier, jnp.where(has_outer, chips + 2, chips + 1))

    def to_sibling(a):
        src, dst = ((tok, x), (cot, dy))[a]
        return pltpu.make_async_remote_copy(
            src_ref=src, dst_ref=dst.at[0, shares(core), :], send_sem=sib_ss.at[a],
            recv_sem=sib_rs.at[a], device_id=sibling, device_id_type=MESH,
        )

    def to_chip(a, q):
        src, dst = ((tok, x), (cot, dy))[a]
        return pltpu.make_async_remote_copy(
            src_ref=src, dst_ref=dst.at[q, shares(core), :], send_sem=ag_ss.at[a, q - 1],
            recv_sem=ag_rs.at[a, q - 1], device_id=partner(q), device_id_type=MESH,
        )

    def forward(a, q):
        ref = (x, dy)[a].at[q, shares(core), :]
        return pltpu.make_async_remote_copy(
            src_ref=ref, dst_ref=ref, send_sem=fw_ss.at[a, q - 1],
            recv_sem=fw_rs.at[a, q - 1], device_id=sibling, device_id_type=MESH,
        )

    for a in range(2):
        to_sibling(a).start()
    for q in range(1, chips):
        for a in range(2):
            to_chip(a, q).start()

    @pl.loop(1, units)
    def _(k):
        for copy in weights(k):
            copy.start()

    def send_inner(t, h):
        ref = part.at[t, :, halves(h), :]
        return pltpu.make_async_remote_copy(
            src_ref=ref, dst_ref=ref, send_sem=p_ss.at[t, h],
            recv_sem=a_rs.at[t, h], device_id=(inner, c), device_id_type=MESH,
        )

    def send_middle(t):
        return pltpu.make_async_remote_copy(
            src_ref=part.at[t, :, halves(given), :], dst_ref=other.at[t], send_sem=p_ss.at[t, given],
            recv_sem=b_rs.at[t], device_id=(inner, c), device_id_type=MESH,
        )

    def share_inner(t, h):
        ref = fin.at[t, :, halves(h), :]
        return pltpu.make_async_remote_copy(
            src_ref=ref, dst_ref=ref, send_sem=fi_ss.at[t],
            recv_sem=f_rs.at[t, h], device_id=(inner, c), device_id_type=MESH,
        )

    def share_outer(t, h):
        ref = fin.at[t, :, halves(h), :]
        return pltpu.make_async_remote_copy(
            src_ref=ref, dst_ref=ref, send_sem=fo_ss.at[t, h],
            recv_sem=f_rs.at[t, h], device_id=(outer, c), device_id_type=MESH,
        )

    def save_xt(q):
        if not turn:
            return pltpu.make_async_copy(x.at[q], xt_out.at[chunks(q), :], xt_s.at[q])
        return pltpu.make_async_copy(xt.at[lax.rem(q, 2)], xt_out.at[:, chunks(q)], xt_s.at[q])

    def save_dy(q):
        return pltpu.make_async_copy(dy.at[q], dy_out.at[chunks(q), :], dy_s.at[q])

    def save_fin(t):
        q, k = lax.div(t, units), lax.rem(t, units)
        return pltpu.make_async_copy(
            fin.at[t, pl.ds(0, 2)], fin_out.at[:, chunks(q), blocks(k)], fin_s.at[t]
        )

    def save_ht(t):
        q, k = lax.div(t, units), lax.rem(t, units)
        if not turn:
            return pltpu.make_async_copy(fin.at[t, 2], ht_out.at[chunks(q), blocks(k)], ht_s.at[t])
        return pltpu.make_async_copy(ht.at[t], ht_out.at[blocks(k), chunks(q)], ht_s.at[t])

    def produce(t):
        q, k = lax.div(t, units), lax.rem(t, units)
        s = lax.rem(t, OWN_SLOTS)

        @pl.when(t == 0)
        def _():
            own_copy(0).wait()
            to_sibling(0).wait_recv()

        @pl.when((k == 0) & (q > 0))
        def _():
            for a in range(2):
                forward(a, q).wait_recv()

        @pl.when(q == 0)
        def _():
            for copy in weights(k):
                copy.wait()

            @pl.loop(0, pieces)
            def _(i):
                at = blocks(i)
                keep = keep_in[k, i].astype(F32)
                w_in[k, 0, at, :] = (w_in[k, 0, at, :].astype(F32) * keep).astype(BF16)
                w_in[k, 1, at, :] = (w_in[k, 1, at, :].astype(F32) * keep).astype(BF16)
                w_dn[k, :, at] = (w_dn[k, :, at].astype(F32) * keep_out[k, i].astype(F32)).astype(BF16)

        own[s, 0] = dot(x[q], w_in[k, 0], ((1,), (0,)))
        own[s, 1] = dot(x[q], w_in[k, 1], ((1,), (0,)))

        @pl.when(t == 0)
        def _():
            own_copy(1).wait()
            to_sibling(1).wait_recv()

        own[s, 2] = dot(dy[q], w_dn[k], ((1,), (1,)))

    def reduce(t):
        s = lax.rem(t, OWN_SLOTS)

        def rounded(h):
            at = halves(h)

            @pl.when(has_outer)
            def _():
                send_inner(t, h).wait_recv()
                for j in range(3):
                    part[t, j, at, :] = (own[s, j, at, :] + part[t, j, at, :].astype(F32)).astype(BF16)

            @pl.when(jnp.logical_not(has_outer))
            def _():
                for j in range(3):
                    part[t, j, at, :] = own[s, j, at, :].astype(BF16)

        rounded(given)

        @pl.when(middle)
        def _():
            send_middle(t).start()

        @pl.when(jnp.logical_not(middle))
        def _():
            send_inner(t, given).start()
            rounded(owned)
            send_inner(t, owned).start()

    def finish(t):
        s = lax.rem(t, OWN_SLOTS)
        at = halves(owned)

        @pl.when(middle)
        def _():
            @pl.when(has_outer)
            def _():
                send_inner(t, owned).wait_recv()
                for j in range(3):
                    own[s, j, at, :] += part[t, j, at, :].astype(F32)

            send_middle(t).wait_recv()
            gate = own[s, 0, at, :] + other[t, 0].astype(F32)
            up = own[s, 1, at, :] + other[t, 1].astype(F32)
            grad = own[s, 2, at, :] + other[t, 2].astype(F32)
            sig = jax.nn.sigmoid(gate)
            act = gate * sig
            fin[t, 0, at, :] = (grad * up * sig * (1.0 + gate * (1.0 - sig))).astype(BF16)
            fin[t, 1, at, :] = (grad * act).astype(BF16)
            fin[t, 2, at, :] = (act * up).astype(BF16)
            share_inner(t, owned).start()

            @pl.when(has_outer)
            def _():
                share_outer(t, owned).start()

    def arrived(t):
        share_inner(t, given).wait_recv()

        @pl.when(has_outer)
        def _():
            share_outer(t, given).start()

        @pl.when(jnp.logical_not(middle))
        def _():
            share_inner(t, owned).wait_recv()

            @pl.when(has_outer)
            def _():
                share_outer(t, owned).start()

    def transpose_tokens(t):
        q, k = lax.div(t, units), lax.rem(t, units)

        if turn:
            @pl.when((k == 0) & (q >= 2))
            def _():
                save_xt(q - 2).wait()

            @pl.loop(lax.div(k * pieces, units), lax.div((k + 1) * pieces, units))
            def _(i):
                xt[lax.rem(q, 2), blocks(i), :] = x[q, :, blocks(i)].T

        @pl.when(k == units - 1)
        def _():
            save_xt(q).start()
            save_dy(q).start()

        @pl.when((k == units // 2) & (q + 1 < chips))
        def _():
            for a in range(2):
                to_chip(a, q + 1).wait_recv()
                forward(a, q + 1).start()

    def to_sibling_sum(q):
        return pltpu.make_async_remote_copy(
            src_ref=acc.at[lax.rem(q, 2), :, shares(1 - core), :], dst_ref=sib.at[q],
            send_sem=rx_ss.at[q], recv_sem=rx_rs.at[q], device_id=sibling, device_id_type=MESH,
        )

    def scatter(q):
        return pltpu.make_async_remote_copy(
            src_ref=rs_send.at[q - 1], dst_ref=rs_recv.at[q - 1], send_sem=rs_ss.at[q - 1],
            recv_sem=rs_rs.at[q - 1], device_id=partner(q), device_id_type=MESH,
        )

    def consume(t):
        q, k = lax.div(t, units), lax.rem(t, units)
        b = lax.rem(q, 2)

        @pl.when(k == 0)
        def _():
            acc[b] = jnp.zeros_like(acc[b])

        save_fin(t).start()
        acc[b, 0] += dot(fin[t, 2], w_dn[k], ((1,), (0,)))
        acc[b, 1] += dot(fin[t, 0], w_in[k, 0], ((1,), (1,))) + dot(
            fin[t, 1], w_in[k, 1], ((1,), (1,))
        )

        @pl.when(k == units - 1)
        def _():
            to_sibling_sum(q).start()

        if turn:
            ht[t] = fin[t, 2].T
        save_ht(t).start()

    def settle(q):
        to_sibling_sum(q).wait()
        at = shares(core)
        for a in range(2):
            sib[q, a] += acc[lax.rem(q, 2), a, at, :]

    @pl.loop(0, count + LAG_USE)
    def _(t):
        @pl.when(t < count)
        def _():
            produce(t)
            reduce(t)

        @pl.when((t >= LAG_OWN) & (t < count + LAG_OWN))
        def _():
            finish(t - LAG_OWN)

        @pl.when(has_outer & (t >= LAG_FWD) & (t < count + LAG_FWD))
        def _():
            arrived(t - LAG_FWD)

        @pl.when(t < count)
        def _():
            transpose_tokens(t)

        @pl.when(t >= LAG_USE)
        def _():
            u = t - LAG_USE

            @pl.when(jnp.logical_not(has_outer))
            def _():
                arrived(u)

            consume(u)
            q = lax.div(u, units) - 1

            @pl.when((lax.rem(u, units) == 1) & (q >= 0))
            def _():
                settle(q)

                @pl.when(q > 0)
                def _():
                    for a in range(2):
                        rs_send[q - 1, a] = sib[q, a].astype(BF16)
                    scatter(q).start()

    last = chips - 1
    for q in range(1, last):
        scatter(q).wait()
        for a in range(2):
            sib[0, a] += rs_recv[q - 1, a].astype(F32)
    save_base = pltpu.make_async_copy(sib.at[0], base, end_s.at[0])
    save_base.start()
    settle(last)
    for a in range(2):
        rs_send[last - 1, a] = sib[last, a].astype(BF16)
    save_tail = pltpu.make_async_copy(rs_send.at[last - 1], tail, end_s.at[1])
    save_tail.start()

    @pl.loop(0, count)
    def _(t):
        save_fin(t).wait()
        save_ht(t).wait()

        @pl.when(middle)
        def _():
            send_middle(t).wait_send()
            share_inner(t, owned).wait_send()

        @pl.when(jnp.logical_not(middle))
        def _():
            for h in range(2):
                send_inner(t, h).wait_send()

        @pl.when(has_outer)
        def _():
            for h in range(2):
                share_outer(t, h).wait_send()

    for a in range(2):
        to_sibling(a).wait_send()
        for q in range(1, chips):
            to_chip(a, q).wait_send()
            forward(a, q).wait_send()
    for q in range(chips):
        save_dy(q).wait()
        if q >= chips - 2 or not turn:
            save_xt(q).wait()
    save_base.wait()
    save_tail.wait()


def wgrad_kernel(
    xt_in, dy_in, fin_in, ht_in, keep_in, keep_out, gate_w, up_w, down_w,
    xt, ht, fin, dy, gate_o, up_o, down_o, order, xt_s, ht_s, fin_s, dy_s, gate_s, up_s, down_s,
):
    pieces = xt.shape[0] // BLOCK
    units = ht.shape[0] // BLOCK

    def blocks(i):
        return pl.ds(pl.multiple_of(i * BLOCK, BLOCK), BLOCK)

    def load_fin(k):
        return pltpu.make_async_copy(fin_in.at[:, :, blocks(k)], fin.at[k], fin_s.at[k])

    def load_dy(i):
        return pltpu.make_async_copy(dy_in.at[:, blocks(i)], dy.at[i], dy_s.at[i])

    def saves(k):
        b = lax.rem(k, 2)
        return (
            pltpu.make_async_copy(gate_o.at[b], gate_w.at[:, blocks(k)], gate_s.at[b]),
            pltpu.make_async_copy(up_o.at[b], up_w.at[:, blocks(k)], up_s.at[b]),
        )

    def save_down(i):
        b = lax.rem(i, 2)
        return pltpu.make_async_copy(down_o.at[b], down_w.at[:, blocks(i)], down_s.at[b])

    load_xt = pltpu.make_async_copy(xt_in, xt, xt_s)
    load_ht = pltpu.make_async_copy(ht_in, ht, ht_s)
    load_fin(0).start()
    load_xt.start()
    load_dy(0).start()
    load_ht.start()

    @pl.loop(1, units)
    def _(k):
        load_fin(k).start()

    @pl.loop(1, pieces)
    def _(i):
        load_dy(i).start()

    def sort(kind, column, length, kept):
        def put(i, n):
            keep = kept(i)
            order[kind, column, jnp.where(keep != 0, n, length - 1 - (i - n))] = i
            return n + keep

        order[kind, column, length] = lax.fori_loop(0, length, put, 0)

    @pl.loop(0, units)
    def _(k):
        sort(0, k, pieces, lambda i: keep_in[k, i])

    @pl.loop(0, pieces)
    def _(i):
        sort(1, i, units, lambda k: keep_out[k, i])

    def products(kind, column, length, left, pairs, kept):
        kept_count = order[kind, column, length]
        step = max(1, length // 4)
        for size in range(step, length + 1, step):
            lowest = kept_count > size - step if size > step else kept_count >= 0

            @pl.when(lowest & (kept_count <= size))
            def _():
                places = [order[kind, column, n] for n in range(length)]
                rows = jnp.concatenate([left[blocks(places[n]), :] for n in range(size)], axis=0)
                for right, out in pairs:
                    whole = dot(rows, right, ((1,), (0,)))
                    for n in range(size):
                        piece = whole[n * BLOCK : (n + 1) * BLOCK]
                        if n >= size - step:
                            piece = piece * kept(places[n]).astype(F32)
                        out[blocks(places[n]), :] = piece.astype(BF16)
                    for n in range(size, length):
                        out[blocks(places[n]), :] = jnp.zeros((BLOCK, BLOCK), BF16)

    def inward(k):
        b = lax.rem(k, 2)
        load_fin(k).wait()

        @pl.when(k >= 2)
        def _():
            for copy in saves(k - 2):
                copy.wait()

        products(
            0, k, pieces, xt, ((fin[k, 0], gate_o.at[b]), (fin[k, 1], up_o.at[b])),
            lambda i: keep_in[k, i],
        )
        for copy in saves(k):
            copy.start()

    def outward(i):
        b = lax.rem(i, 2)
        load_dy(i).wait()

        @pl.when(i >= 2)
        def _():
            save_down(i - 2).wait()

        products(1, i, units, ht, ((dy[i], down_o.at[b]),), lambda k: keep_out[k, i])
        save_down(i).start()

    load_xt.wait()

    @pl.loop(0, max(units, pieces))
    def _(n):
        @pl.when(n < units)
        def _():
            inward(n)

        @pl.when(n == 0)
        def _():
            load_ht.wait()

        @pl.when(n < pieces)
        def _():
            outward(n)

    for k in range(max(0, units - 2), units):
        for copy in saves(k):
            copy.wait()
    for i in range(max(0, pieces - 2), pieces):
        save_down(i).wait()


def weight_grads(xt, dy, fin, ht, mask_in, mask_out):
    width, total = xt.shape
    hidden = ht.shape[0]
    pieces, units = width // BLOCK, hidden // BLOCK
    struct = jax.ShapeDtypeStruct
    smem = pl.BlockSpec(memory_space=pltpu.SMEM)
    anywhere = pl.BlockSpec(memory_space=pl.ANY)
    dma = pltpu.SemaphoreType.DMA
    return pl.pallas_call(
        wgrad_kernel,
        out_shape=(
            struct((width, hidden), BF16),
            struct((width, hidden), BF16),
            struct((hidden, width), BF16),
        ),
        in_specs=[anywhere] * 4 + [smem] * 2,
        out_specs=(anywhere,) * 3,
        scratch_shapes=[
            pltpu.VMEM((width, total), BF16),
            pltpu.VMEM((hidden, total), BF16),
            pltpu.VMEM((units, 2, total, BLOCK), BF16),
            pltpu.VMEM((pieces, total, BLOCK), BF16),
            pltpu.VMEM((2, width, BLOCK), BF16),
            pltpu.VMEM((2, width, BLOCK), BF16),
            pltpu.VMEM((2, hidden, BLOCK), BF16),
            pltpu.SMEM((2, max(units, pieces), max(units, pieces) + 1), jnp.int32),
            dma, dma, dma((units,)), dma((pieces,)), dma((2,)), dma((2,)), dma((2,)),
        ],
        compiler_params=pltpu.CompilerParams(vmem_limit_bytes=60 * 1024 * 1024),
        cost_estimate=pl.CostEstimate(
            flops=6 * total * width * hidden,
            bytes_accessed=6 * width * hidden + 10 * total * width,
            transcendentals=0,
        ),
        name="wgrad",
    )(xt, dy, fin, ht, mask_in, mask_out)


def local(rows, cols, tokens, w_gate, w_up, w_down, mask_in, mask_out, out_grad):
    share, width = tokens.shape
    hidden = w_gate.shape[1]
    units = hidden // BLOCK
    total = share * cols
    chips = cols // CORES
    chunk = CORES * share
    count = chips * units
    smem = pl.BlockSpec(memory_space=pltpu.SMEM)
    anywhere = pl.BlockSpec(memory_space=pl.ANY)
    dma = pltpu.SemaphoreType.DMA
    struct = jax.ShapeDtypeStruct
    base, tail, xt, dy, fin, ht = pl.pallas_call(
        functools.partial(step_kernel, rows, cols, units),
        out_shape=(
            struct((2, share, width), F32),
            struct((2, share, width), BF16),
            struct((width, total) if turned(chunk) else (total, width), BF16),
            struct((total, width), BF16),
            struct((2, total, hidden), BF16),
            struct((hidden, total) if turned(chunk) else (total, hidden), BF16),
        ),
        in_specs=[anywhere] * 5 + [smem] * 2,
        out_specs=(anywhere,) * 6,
        scratch_shapes=[
            pltpu.VMEM((chips, chunk, width), BF16),
            pltpu.VMEM((chips, chunk, width), BF16),
            pltpu.VMEM((2, width, chunk), BF16),
            pltpu.VMEM((count, 3, chunk, BLOCK), BF16),
            pltpu.VMEM((count, 3, chunk // 2, BLOCK), BF16),
            pltpu.VMEM((count, 3, chunk, BLOCK), BF16),
            pltpu.VMEM((count, BLOCK, chunk) if turned(chunk) else (1, 16, 128), BF16),
            pltpu.VMEM((OWN_SLOTS, 3, chunk, BLOCK), F32),
            pltpu.VMEM((units, 2, width, BLOCK), BF16),
            pltpu.VMEM((units, BLOCK, width), BF16),
            pltpu.VMEM((2, 2, chunk, width), F32),
            pltpu.VMEM((chips, 2, share, width), F32),
            pltpu.VMEM((chips - 1, 2, share, width), BF16),
            pltpu.VMEM((chips - 2, 2, share, width), BF16),
            dma((2,)), dma((2,)), dma((2,)),
            dma((2, chips - 1)), dma((2, chips - 1)),
            dma((2, chips - 1)), dma((2, chips - 1)),
            dma((units, 3)),
            dma((count, 2)), dma((count, 2)), dma((count,)),
            dma((count,)), dma((count, 2)), dma((count, 2)),
            dma((chips,)), dma((chips,)), dma((count,)), dma((count,)),
            dma((chips,)), dma((chips,)),
            dma((chips - 2,)), dma((chips - 2,)),
            dma((2,)),
        ],
        compiler_params=pltpu.CompilerParams(
            collective_id=0, has_side_effects=True, vmem_limit_bytes=63 * 1024 * 1024
        ),
        cost_estimate=pl.CostEstimate(
            flops=12 * total * width * hidden,
            bytes_accessed=6 * width * hidden,
            transcendentals=total * hidden,
        ),
        name="step",
    )(tokens, out_grad, w_gate, w_up, w_down, mask_in, mask_out)
    if not turned(chunk):
        xt, ht = xt.T, ht.T
    nearest = [(i, (i // CORES ^ 1) * CORES + i % CORES) for i in range(cols)]
    moved = lax.ppermute(tail, "col", nearest)
    gate_wgrad, up_wgrad, down_wgrad = weight_grads(xt, dy, fin, ht, mask_in, mask_out)
    result = (base + moved.astype(F32)).astype(BF16)
    return result[0], result[1], gate_wgrad, up_wgrad, down_wgrad


def solution(mesh):
    placed = (
        P("col", "row"),
        P("row", "col"),
        P("row", "col"),
        P("col", "row"),
        P("col", "row"),
        P("col", "row"),
        P("col", "row"),
    )
    return jax.shard_map(
        functools.partial(local, mesh.shape["row"], mesh.shape["col"]),
        mesh=mesh,
        in_specs=placed,
        out_specs=(
            P("col", "row"),
            P("col", "row"),
            P("row", "col"),
            P("row", "col"),
            P("col", "row"),
        ),
        check_vma=False,
    )
```

```python
import functools

import jax
import jax.numpy as jnp
from jax import lax
from jax.experimental import pallas as pl
from jax.experimental.pallas import tpu as pltpu
from jax.sharding import PartitionSpec as P

BLOCK = 256
CORES = 2
LAG_OWN = 1
LAG_FWD = 2
LAG_USE = 5
OWN_SLOTS = LAG_OWN + 1
KEPT = 10
SAVED = 3
SPLIT = 1
MESH = pl.DeviceIdType.MESH
F32 = jnp.float32
BF16 = jnp.bfloat16


def dot(left, right, dims):
    return lax.dot_general(left, right, (dims, ((), ())), preferred_element_type=F32)


def turned(chunk):
    return chunk % 128 == 0


def flip(chip, j, chips):
    other, bit = chip, 1
    while bit < chips:
        other = other + lax.rem(lax.div(j, bit), 2) * (bit - 2 * bit * lax.rem(lax.div(chip, bit), 2))
        bit *= 2
    return other


def place(q, chips):
    return jnp.where(q == 0, 0, jnp.where(q == chips - 1, 1, q + 1))


def step_kernel(
    rows, cols, units,
    tok, cot, w_gate, w_up, w_down, mask_in, mask_out,
    base, tail, xt_out, dy_out, fin_out, ht_out,
    x, dy, xt, part, other, fin, ht, own, w_in, w_dn, acc, sib, rs_send, rs_recv,
    keep_in, keep_out, keep_s,
    own_s, sib_ss, sib_rs, ag_ss, ag_rs, fw_ss, fw_rs, w_s, p_ss, a_rs, b_rs, fi_ss, fo_ss, f_rs,
    xt_s, dy_s, fin_s, ht_s, rx_ss, rx_rs, rs_ss, rs_rs, end_s,
):
    r = lax.axis_index("row")
    c = lax.axis_index("col")
    chips = cols // CORES
    chip, core = lax.div(c, CORES), lax.rem(c, CORES)
    low = r < rows // 2
    inner = jnp.where(low, r + 1, r - 1)
    outer = jnp.where(low, r - 1, r + 1)
    has_outer = (r > 0) & (r < rows - 1)
    middle = (r == rows // 2 - 1) | (r == rows // 2)
    owned = jnp.where(low, 0, 1)
    given = 1 - owned
    share, width = tok.shape
    chunk = CORES * share
    half = chunk // 2
    split = max(1, min(SPLIT, half // 16))
    part_rows = half // split
    pieces = width // BLOCK
    count = chips * units
    last = chips - 1
    turn = turned(chunk)
    sibling = (r, chip * CORES + (1 - core))

    def partner(q):
        return (r, flip(chip, place(q, chips), chips) * CORES + core)

    def rows_of(h, u):
        return pl.ds(pl.multiple_of(h * half + u * part_rows, part_rows), part_rows)

    def shares(e):
        return pl.ds(pl.multiple_of(e * share, share), share)

    def blocks(i):
        return pl.ds(pl.multiple_of(i * BLOCK, BLOCK), BLOCK)

    def chunks(q):
        return pl.ds(pl.multiple_of(q * chunk, chunk), chunk)

    def weights(k):
        return (
            pltpu.make_async_copy(w_gate.at[:, blocks(k)], w_in.at[k, 0], w_s.at[k, 0]),
            pltpu.make_async_copy(w_up.at[:, blocks(k)], w_in.at[k, 1], w_s.at[k, 1]),
            pltpu.make_async_copy(w_down.at[blocks(k), :], w_dn.at[k], w_s.at[k, 2]),
        )

    def own_copy(a):
        src, dst = ((tok, x), (cot, dy))[a]
        return pltpu.make_async_copy(src, dst.at[0, shares(core), :], own_s.at[a])

    masks = [
        pltpu.make_async_copy(mask_in, keep_in, keep_s.at[0]),
        pltpu.make_async_copy(mask_out, keep_out, keep_s.at[1]),
    ]
    for copy in masks:
        copy.start()
    for copy in weights(0):
        copy.start()
    for a in range(2):
        own_copy(a).start()

    barrier = pltpu.get_barrier_semaphore()
    pl.semaphore_signal(barrier, inc=1, device_id=(inner, c), device_id_type=MESH)
    pl.semaphore_signal(barrier, inc=1, device_id=sibling, device_id_type=MESH)
    for q in range(1, chips):
        pl.semaphore_signal(barrier, inc=1, device_id=partner(q), device_id_type=MESH)

    @pl.when(has_outer)
    def _():
        pl.semaphore_signal(barrier, inc=1, device_id=(outer, c), device_id_type=MESH)

    def prepare(k):
        for copy in weights(k):
            copy.wait()

        @pl.loop(0, pieces)
        def _(i):
            at = blocks(i)
            keep = keep_in[k, i].astype(F32)
            w_in[k, 0, at, :] = (w_in[k, 0, at, :].astype(F32) * keep).astype(BF16)
            w_in[k, 1, at, :] = (w_in[k, 1, at, :].astype(F32) * keep).astype(BF16)
            w_dn[k, :, at] = (w_dn[k, :, at].astype(F32) * keep_out[k, i].astype(F32)).astype(BF16)

    for copy in masks:
        copy.wait()
    prepare(0)
    pl.semaphore_wait(barrier, jnp.where(has_outer, chips + 2, chips + 1))

    def to_sibling(a):
        src, dst = ((tok, x), (cot, dy))[a]
        return pltpu.make_async_remote_copy(
            src_ref=src, dst_ref=dst.at[0, shares(core), :], send_sem=sib_ss.at[a],
            recv_sem=sib_rs.at[a], device_id=sibling, device_id_type=MESH,
        )

    def to_chip(a, q):
        src, dst = ((tok, x), (cot, dy))[a]
        return pltpu.make_async_remote_copy(
            src_ref=src, dst_ref=dst.at[q, shares(core), :], send_sem=ag_ss.at[a, q - 1],
            recv_sem=ag_rs.at[a, q - 1], device_id=partner(q), device_id_type=MESH,
        )

    def forward(a, q):
        ref = (x, dy)[a].at[q, shares(core), :]
        return pltpu.make_async_remote_copy(
            src_ref=ref, dst_ref=ref, send_sem=fw_ss.at[a, q - 1],
            recv_sem=fw_rs.at[a, q - 1], device_id=sibling, device_id_type=MESH,
        )

    for a in range(2):
        to_sibling(a).start()
    for q in range(1, chips):
        for a in range(2):
            to_chip(a, q).start()

    @pl.loop(1, units)
    def _(k):
        for copy in weights(k):
            copy.start()

    def send_inner(t, h, u):
        ref = part.at[t, :, rows_of(h, u), :]
        return pltpu.make_async_remote_copy(
            src_ref=ref, dst_ref=ref, send_sem=p_ss.at[t, h, u],
            recv_sem=a_rs.at[t, h, u], device_id=(inner, c), device_id_type=MESH,
        )

    def send_middle(t, u):
        return pltpu.make_async_remote_copy(
            src_ref=part.at[t, :, rows_of(given, u), :], dst_ref=other.at[t, :, rows_of(0, u), :],
            send_sem=p_ss.at[t, given, u], recv_sem=b_rs.at[t, u], device_id=(inner, c), device_id_type=MESH,
        )

    def share_inner(t, h, u):
        ref = fin.at[t, :, rows_of(h, u), :]
        return pltpu.make_async_remote_copy(
            src_ref=ref, dst_ref=ref, send_sem=fi_ss.at[t, u],
            recv_sem=f_rs.at[t, h, u], device_id=(inner, c), device_id_type=MESH,
        )

    def share_outer(t, h, u):
        ref = fin.at[t, :, rows_of(h, u), :]
        return pltpu.make_async_remote_copy(
            src_ref=ref, dst_ref=ref, send_sem=fo_ss.at[t, h, u],
            recv_sem=f_rs.at[t, h, u], device_id=(outer, c), device_id_type=MESH,
        )

    def save_xt(q):
        if not turn:
            return pltpu.make_async_copy(x.at[q], xt_out.at[chunks(q), :], xt_s.at[q])
        return pltpu.make_async_copy(xt.at[lax.rem(q, 2)], xt_out.at[:, chunks(q)], xt_s.at[q])

    def save_dy(q):
        return pltpu.make_async_copy(dy.at[q], dy_out.at[chunks(q), :], dy_s.at[q])

    def save_fin(t):
        q, k = lax.div(t, units), lax.rem(t, units)
        return pltpu.make_async_copy(
            fin.at[t, pl.ds(0, 2)], fin_out.at[:, chunks(q), blocks(k)], fin_s.at[t]
        )

    def save_ht(t):
        q, k = lax.div(t, units), lax.rem(t, units)
        if not turn:
            return pltpu.make_async_copy(fin.at[t, 2], ht_out.at[chunks(q), blocks(k)], ht_s.at[t])
        return pltpu.make_async_copy(ht.at[t], ht_out.at[blocks(k), chunks(q)], ht_s.at[t])

    def produce(t):
        q, k = lax.div(t, units), lax.rem(t, units)
        s = lax.rem(t, OWN_SLOTS)

        @pl.when(t == 0)
        def _():
            own_copy(0).wait()
            to_sibling(0).wait_recv()

        @pl.when((k == 0) & (q > 0))
        def _():
            for a in range(2):
                forward(a, q).wait_recv()

        @pl.when((q == 0) & (k > 0))
        def _():
            prepare(k)

        own[s, 0] = dot(x[q], w_in[k, 0], ((1,), (0,)))
        own[s, 1] = dot(x[q], w_in[k, 1], ((1,), (0,)))

        @pl.when(t == 0)
        def _():
            own_copy(1).wait()
            to_sibling(1).wait_recv()

        own[s, 2] = dot(dy[q], w_dn[k], ((1,), (1,)))

    def reduce(t):
        s = lax.rem(t, OWN_SLOTS)

        def rounded(h, u):
            at = rows_of(h, u)

            @pl.when(has_outer)
            def _():
                send_inner(t, h, u).wait_recv()
                for j in range(3):
                    part[t, j, at, :] = (own[s, j, at, :] + part[t, j, at, :].astype(F32)).astype(BF16)

            @pl.when(jnp.logical_not(has_outer))
            def _():
                for j in range(3):
                    part[t, j, at, :] = own[s, j, at, :].astype(BF16)

        @pl.loop(0, split)
        def _(u):
            rounded(given, u)

            @pl.when(middle)
            def _():
                send_middle(t, u).start()

            @pl.when(jnp.logical_not(middle))
            def _():
                send_inner(t, given, u).start()

        @pl.when(jnp.logical_not(middle))
        def _():
            @pl.loop(0, split)
            def _(u):
                rounded(owned, u)
                send_inner(t, owned, u).start()

    def finish(t):
        s = lax.rem(t, OWN_SLOTS)

        def one(u):
            at = rows_of(owned, u)
            there = rows_of(0, u)

            @pl.when(has_outer)
            def _():
                send_inner(t, owned, u).wait_recv()
                for j in range(3):
                    own[s, j, at, :] += part[t, j, at, :].astype(F32)

            send_middle(t, u).wait_recv()
            gate = own[s, 0, at, :] + other[t, 0, there, :].astype(F32)
            up = own[s, 1, at, :] + other[t, 1, there, :].astype(F32)
            grad = own[s, 2, at, :] + other[t, 2, there, :].astype(F32)
            sig = jax.nn.sigmoid(gate)
            act = gate * sig
            fin[t, 0, at, :] = (grad * up * sig * (1.0 + gate * (1.0 - sig))).astype(BF16)
            fin[t, 1, at, :] = (grad * act).astype(BF16)
            fin[t, 2, at, :] = (act * up).astype(BF16)

            share_inner(t, owned, u).start()

            @pl.when(has_outer)
            def _():
                share_outer(t, owned, u).start()

        @pl.when(middle)
        def _():
            pl.loop(0, split)(one)

    def arrived(t):
        def one(h, u):
            share_inner(t, h, u).wait_recv()

            @pl.when(has_outer)
            def _():
                share_outer(t, h, u).start()

        @pl.loop(0, split)
        def _(u):
            one(given, u)

            @pl.when(jnp.logical_not(middle))
            def _():
                one(owned, u)

    def transpose_tokens(t):
        q, k = lax.div(t, units), lax.rem(t, units)

        if turn:
            @pl.when((k == 0) & (q >= 2))
            def _():
                save_xt(q - 2).wait()

            @pl.loop(lax.div(k * pieces, units), lax.div((k + 1) * pieces, units))
            def _(i):
                xt[lax.rem(q, 2), blocks(i), :] = x[q, :, blocks(i)].T

        @pl.when(k == units - 1)
        def _():
            save_xt(q).start()
            save_dy(q).start()

        @pl.when((k == units // 2) & (q + 1 < chips))
        def _():
            for a in range(2):
                to_chip(a, q + 1).wait_recv()
                forward(a, q + 1).start()

    def to_sibling_sum(q, a):
        return pltpu.make_async_remote_copy(
            src_ref=acc.at[lax.rem(q, 2), a, shares(1 - core), :], dst_ref=sib.at[q, a],
            send_sem=rx_ss.at[q, a], recv_sem=rx_rs.at[q, a], device_id=sibling, device_id_type=MESH,
        )

    def scatter(q):
        return pltpu.make_async_remote_copy(
            src_ref=rs_send.at[q - 1], dst_ref=rs_recv.at[q - 1], send_sem=rs_ss.at[q - 1],
            recv_sem=rs_rs.at[q - 1], device_id=partner(q), device_id_type=MESH,
        )

    def consume(t):
        q, k = lax.div(t, units), lax.rem(t, units)
        b = lax.rem(q, 2)

        @pl.when(k == 0)
        def _():
            acc[b] = jnp.zeros_like(acc[b])

        save_fin(t).start()
        acc[b, 0] += dot(fin[t, 2], w_dn[k], ((1,), (0,)))

        @pl.when(k == units - 1)
        def _():
            to_sibling_sum(q, 0).start()

        acc[b, 1] += dot(fin[t, 0], w_in[k, 0], ((1,), (1,))) + dot(
            fin[t, 1], w_in[k, 1], ((1,), (1,))
        )

        @pl.when(k == units - 1)
        def _():
            to_sibling_sum(q, 1).start()

        if turn:
            ht[t] = fin[t, 2].T
        save_ht(t).start()

    def sent(t):
        @pl.loop(0, split)
        def _(u):
            @pl.when(middle)
            def _():
                send_middle(t, u).wait_send()
                share_inner(t, owned, u).wait_send()

            @pl.when(jnp.logical_not(middle))
            def _():
                for h in range(2):
                    send_inner(t, h, u).wait_send()

            @pl.when(has_outer)
            def _():
                for h in range(2):
                    share_outer(t, h, u).wait_send()

    def saved(t):
        save_fin(t).wait()
        save_ht(t).wait()

    def gathered():
        for a in range(2):
            to_sibling(a).wait_send()
            for q in range(1, chips):
                to_chip(a, q).wait_send()
                forward(a, q).wait_send()
        for q in range(last):
            save_dy(q).wait()
            if q < last - 1 and turn:
                continue
            save_xt(q).wait()

    def settle(q):
        at = shares(core)
        for a in range(2):
            to_sibling_sum(q, a).wait()
            sib[q, a] += acc[lax.rem(q, 2), a, at, :]

    @pl.loop(0, count + LAG_USE)
    def _(t):
        @pl.when(t < count)
        def _():
            produce(t)
            reduce(t)

        @pl.when((t >= LAG_OWN) & (t < count + LAG_OWN))
        def _():
            finish(t - LAG_OWN)

        @pl.when(has_outer & (t >= LAG_FWD) & (t < count + LAG_FWD))
        def _():
            arrived(t - LAG_FWD)

        @pl.when(t < count)
        def _():
            transpose_tokens(t)

        @pl.when((t >= KEPT) & (t < count + KEPT))
        def _():
            sent(t - KEPT)

        @pl.when(t == count - 1)
        def _():
            gathered()

        @pl.when(t >= LAG_USE)
        def _():
            u = t - LAG_USE

            @pl.when(jnp.logical_not(has_outer))
            def _():
                arrived(u)

            consume(u)

            @pl.when(u >= SAVED)
            def _():
                saved(u - SAVED)

            q = lax.div(u, units) - 1

            @pl.when((lax.rem(u, units) == 1) & (q >= 0))
            def _():
                settle(q)

                @pl.when(q > 0)
                def _():
                    for a in range(2):
                        rs_send[q - 1, a] = sib[q, a].astype(BF16)
                    scatter(q).start()

    for q in range(1, last):
        scatter(q).wait()
        for a in range(2):
            sib[0, a] += rs_recv[q - 1, a].astype(F32)
    save_base = pltpu.make_async_copy(sib.at[0], base, end_s.at[0])
    save_base.start()
    for a in range(2):
        to_sibling_sum(last, a).wait()
        rs_send[last - 1, a] = (sib[last, a] + acc[last % 2, a, shares(core), :]).astype(BF16)
    save_tail = pltpu.make_async_copy(rs_send.at[last - 1], tail, end_s.at[1])
    save_tail.start()

    @pl.loop(max(0, count - SAVED), count)
    def _(t):
        saved(t)

    @pl.loop(max(0, count + LAG_USE - KEPT), count)
    def _(t):
        sent(t)

    save_dy(last).wait()
    save_xt(last).wait()
    save_base.wait()
    save_tail.wait()


def wgrad_kernel(
    xt_in, dy_in, fin_in, ht_in, mask_in, mask_out, gate_w, up_w, down_w,
    xt, ht, fin, dy, gate_o, up_o, down_o, order, keep_in, keep_out, keep_s, xt_s, ht_s, fin_s, dy_s, gate_s, up_s, down_s,
):
    pieces = xt.shape[0] // BLOCK
    units = ht.shape[0] // BLOCK

    def blocks(i):
        return pl.ds(pl.multiple_of(i * BLOCK, BLOCK), BLOCK)

    def load_fin(k):
        return pltpu.make_async_copy(fin_in.at[:, :, blocks(k)], fin.at[k], fin_s.at[k])

    def load_dy(i):
        return pltpu.make_async_copy(dy_in.at[:, blocks(i)], dy.at[i], dy_s.at[i])

    def saves(k):
        b = lax.rem(k, 2)
        return (
            pltpu.make_async_copy(gate_o.at[b], gate_w.at[:, blocks(k)], gate_s.at[b]),
            pltpu.make_async_copy(up_o.at[b], up_w.at[:, blocks(k)], up_s.at[b]),
        )

    def save_down(i):
        b = lax.rem(i, 2)
        return pltpu.make_async_copy(down_o.at[b], down_w.at[:, blocks(i)], down_s.at[b])

    masks = [
        pltpu.make_async_copy(mask_in, keep_in, keep_s.at[0]),
        pltpu.make_async_copy(mask_out, keep_out, keep_s.at[1]),
    ]
    load_xt = pltpu.make_async_copy(xt_in, xt, xt_s)
    load_ht = pltpu.make_async_copy(ht_in, ht, ht_s)
    load_fin(0).start()
    load_xt.start()
    for copy in masks:
        copy.start()
    load_dy(0).start()
    load_ht.start()

    @pl.loop(1, units)
    def _(k):
        load_fin(k).start()

    @pl.loop(1, pieces)
    def _(i):
        load_dy(i).start()

    def sort(kind, column, length, kept):
        def put(i, n):
            keep = kept(i)
            order[kind, column, jnp.where(keep != 0, n, length - 1 - (i - n))] = i
            return n + keep

        order[kind, column, length] = lax.fori_loop(0, length, put, 0)

    for copy in masks:
        copy.wait()

    @pl.loop(0, units)
    def _(k):
        sort(0, k, pieces, lambda i: keep_in[k, i])

    @pl.loop(0, pieces)
    def _(i):
        sort(1, i, units, lambda k: keep_out[k, i])

    def products(kind, column, length, left, pairs, kept):
        kept_count = order[kind, column, length]
        step = max(1, length // 8)
        for size in range(step, length + 1, step):
            lowest = kept_count > size - step if size > step else kept_count >= 0

            @pl.when(lowest & (kept_count <= size))
            def _():
                places = [order[kind, column, n] for n in range(length)]
                rows = jnp.concatenate([left[blocks(places[n]), :] for n in range(size)], axis=0)
                for right, out in pairs:
                    whole = dot(rows, right, ((1,), (0,)))
                    for n in range(size):
                        piece = whole[n * BLOCK : (n + 1) * BLOCK]
                        if n >= size - step:
                            piece = piece * kept(places[n]).astype(F32)
                        out[blocks(places[n]), :] = piece.astype(BF16)
                    for n in range(size, length):
                        out[blocks(places[n]), :] = jnp.zeros((BLOCK, BLOCK), BF16)

    def inward(k):
        b = lax.rem(k, 2)
        load_fin(k).wait()

        @pl.when(k >= 2)
        def _():
            for copy in saves(k - 2):
                copy.wait()

        products(
            0, k, pieces, xt, ((fin[k, 0], gate_o.at[b]), (fin[k, 1], up_o.at[b])),
            lambda i: keep_in[k, i],
        )
        for copy in saves(k):
            copy.start()

    def outward(i):
        b = lax.rem(i, 2)
        load_dy(i).wait()

        @pl.when(i >= 2)
        def _():
            save_down(i - 2).wait()

        products(1, i, units, ht, ((dy[i], down_o.at[b]),), lambda k: keep_out[k, i])
        save_down(i).start()

    load_xt.wait()

    @pl.loop(0, max(units, pieces))
    def _(n):
        @pl.when(n < units)
        def _():
            inward(n)

        @pl.when(n == 0)
        def _():
            load_ht.wait()

        @pl.when(n < pieces)
        def _():
            outward(n)

    for k in range(max(0, units - 2), units):
        for copy in saves(k):
            copy.wait()
    for i in range(max(0, pieces - 2), pieces):
        save_down(i).wait()


def weight_grads(xt, dy, fin, ht, mask_in, mask_out):
    width, total = xt.shape
    hidden = ht.shape[0]
    pieces, units = width // BLOCK, hidden // BLOCK
    struct = jax.ShapeDtypeStruct
    anywhere = pl.BlockSpec(memory_space=pl.ANY)
    dma = pltpu.SemaphoreType.DMA
    return pl.pallas_call(
        wgrad_kernel,
        out_shape=(
            struct((width, hidden), BF16),
            struct((width, hidden), BF16),
            struct((hidden, width), BF16),
        ),
        in_specs=[anywhere] * 6,
        out_specs=(anywhere,) * 3,
        scratch_shapes=[
            pltpu.VMEM((width, total), BF16),
            pltpu.VMEM((hidden, total), BF16),
            pltpu.VMEM((units, 2, total, BLOCK), BF16),
            pltpu.VMEM((pieces, total, BLOCK), BF16),
            pltpu.VMEM((2, width, BLOCK), BF16),
            pltpu.VMEM((2, width, BLOCK), BF16),
            pltpu.VMEM((2, hidden, BLOCK), BF16),
            pltpu.SMEM((2, max(units, pieces), max(units, pieces) + 1), jnp.int32),
            pltpu.SMEM((units, pieces), jnp.int32),
            pltpu.SMEM((units, pieces), jnp.int32),
            dma((2,)),
            dma, dma, dma((units,)), dma((pieces,)), dma((2,)), dma((2,)), dma((2,)),
        ],
        compiler_params=pltpu.CompilerParams(vmem_limit_bytes=60 * 1024 * 1024),
        cost_estimate=pl.CostEstimate(
            flops=6 * total * width * hidden,
            bytes_accessed=6 * width * hidden + 10 * total * width,
            transcendentals=0,
        ),
        name="wgrad",
    )(xt, dy, fin, ht, mask_in, mask_out)


def local(rows, cols, tokens, w_gate, w_up, w_down, mask_in, mask_out, out_grad):
    share, width = tokens.shape
    hidden = w_gate.shape[1]
    units = hidden // BLOCK
    total = share * cols
    chips = cols // CORES
    chunk = CORES * share
    count = chips * units
    anywhere = pl.BlockSpec(memory_space=pl.ANY)
    dma = pltpu.SemaphoreType.DMA
    struct = jax.ShapeDtypeStruct
    base, tail, xt, dy, fin, ht = pl.pallas_call(
        functools.partial(step_kernel, rows, cols, units),
        out_shape=(
            struct((2, share, width), F32),
            struct((2, share, width), BF16),
            struct((width, total) if turned(chunk) else (total, width), BF16),
            struct((total, width), BF16),
            struct((2, total, hidden), BF16),
            struct((hidden, total) if turned(chunk) else (total, hidden), BF16),
        ),
        in_specs=[anywhere] * 7,
        out_specs=(anywhere,) * 6,
        scratch_shapes=[
            pltpu.VMEM((chips, chunk, width), BF16),
            pltpu.VMEM((chips, chunk, width), BF16),
            pltpu.VMEM((2, width, chunk), BF16),
            pltpu.VMEM((count, 3, chunk, BLOCK), BF16),
            pltpu.VMEM((count, 3, chunk // 2, BLOCK), BF16),
            pltpu.VMEM((count, 3, chunk, BLOCK), BF16),
            pltpu.VMEM((count, BLOCK, chunk) if turned(chunk) else (1, 16, 128), BF16),
            pltpu.VMEM((OWN_SLOTS, 3, chunk, BLOCK), F32),
            pltpu.VMEM((units, 2, width, BLOCK), BF16),
            pltpu.VMEM((units, BLOCK, width), BF16),
            pltpu.VMEM((2, 2, chunk, width), F32),
            pltpu.VMEM((chips, 2, share, width), F32),
            pltpu.VMEM((chips - 1, 2, share, width), BF16),
            pltpu.VMEM((chips - 2, 2, share, width), BF16),
            pltpu.SMEM((units, width // BLOCK), jnp.int32),
            pltpu.SMEM((units, width // BLOCK), jnp.int32),
            dma((2,)),
            dma((2,)), dma((2,)), dma((2,)),
            dma((2, chips - 1)), dma((2, chips - 1)),
            dma((2, chips - 1)), dma((2, chips - 1)),
            dma((units, 3)),
            dma((count, 2, SPLIT)), dma((count, 2, SPLIT)), dma((count, SPLIT)),
            dma((count, SPLIT)), dma((count, 2, SPLIT)), dma((count, 2, SPLIT)),
            dma((chips,)), dma((chips,)), dma((count,)), dma((count,)),
            dma((chips, 2)), dma((chips, 2)),
            dma((chips - 2,)), dma((chips - 2,)),
            dma((2,)),
        ],
        compiler_params=pltpu.CompilerParams(
            collective_id=0, has_side_effects=True, vmem_limit_bytes=63 * 1024 * 1024
        ),
        cost_estimate=pl.CostEstimate(
            flops=12 * total * width * hidden,
            bytes_accessed=6 * width * hidden,
            transcendentals=total * hidden,
        ),
        name="step",
    )(tokens, out_grad, w_gate, w_up, w_down, mask_in, mask_out)
    if not turned(chunk):
        xt, ht = xt.T, ht.T
    nearest = [(i, (i // CORES ^ 1) * CORES + i % CORES) for i in range(cols)]
    moved = lax.ppermute(tail, "col", nearest)
    gate_wgrad, up_wgrad, down_wgrad = weight_grads(xt, dy, fin, ht, mask_in, mask_out)
    output, tokens_grad = [(base[a] + moved[a].astype(F32)).astype(BF16) for a in range(2)]
    return output, tokens_grad, gate_wgrad, up_wgrad, down_wgrad


def solution(mesh):
    placed = (
        P("col", "row"),
        P("row", "col"),
        P("row", "col"),
        P("col", "row"),
        P("col", "row"),
        P("col", "row"),
        P("col", "row"),
    )
    return jax.shard_map(
        functools.partial(local, mesh.shape["row"], mesh.shape["col"]),
        mesh=mesh,
        in_specs=placed,
        out_specs=(
            P("col", "row"),
            P("col", "row"),
            P("row", "col"),
            P("row", "col"),
            P("col", "row"),
        ),
        check_vma=False,
    )
```

```python
import functools

import jax
import jax.numpy as jnp
from jax import lax
from jax.experimental import pallas as pl
from jax.experimental.pallas import tpu as pltpu
from jax.sharding import PartitionSpec as P

BLOCK = 256
CORES = 2
LAG_OWN = 1
LAG_FWD = 2
LAG_USE = 5
OWN_SLOTS = LAG_OWN + 1
KEPT = 10
SAVED = 3
SPLIT = 1
MESH = pl.DeviceIdType.MESH
F32 = jnp.float32
BF16 = jnp.bfloat16


def dot(left, right, dims):
    return lax.dot_general(left, right, (dims, ((), ())), preferred_element_type=F32)


def turned(chunk):
    return chunk % 128 == 0


def flip(chip, j, chips):
    other, bit = chip, 1
    while bit < chips:
        other = other + lax.rem(lax.div(j, bit), 2) * (bit - 2 * bit * lax.rem(lax.div(chip, bit), 2))
        bit *= 2
    return other


def place(q, chips):
    return jnp.where(q == 0, 0, jnp.where(q == chips - 1, 1, q + 1))


def step_kernel(
    rows, cols, units,
    tok, cot, w_gate, w_up, w_down, mask_in, mask_out,
    base, tail, xt_out, dy_out, fin_out, ht_out,
    x, dy, xt, part, other, fin, ht, own, w_in, w_dn, acc, sib, rs_send, rs_recv,
    keep_in, keep_out, keep_s,
    own_s, sib_ss, sib_rs, ag_ss, ag_rs, fw_ss, fw_rs, w_s, p_ss, a_rs, b_rs, fi_ss, fo_ss, f_rs,
    xt_s, dy_s, fin_s, ht_s, rx_ss, rx_rs, rs_ss, rs_rs, end_s,
):
    r = lax.axis_index("row")
    c = lax.axis_index("col")
    chips = cols // CORES
    chip, core = lax.div(c, CORES), lax.rem(c, CORES)
    low = r < rows // 2
    inner = jnp.where(low, r + 1, r - 1)
    outer = jnp.where(low, r - 1, r + 1)
    has_outer = (r > 0) & (r < rows - 1)
    middle = (r == rows // 2 - 1) | (r == rows // 2)
    owned = jnp.where(low, 0, 1)
    given = 1 - owned
    share, width = tok.shape
    chunk = CORES * share
    half = chunk // 2
    split = max(1, min(SPLIT, half // 16))
    part_rows = half // split
    pieces = width // BLOCK
    count = chips * units
    last = chips - 1
    turn = turned(chunk)
    sibling = (r, chip * CORES + (1 - core))

    def partner(q):
        return (r, flip(chip, place(q, chips), chips) * CORES + core)

    def rows_of(h, u):
        return pl.ds(pl.multiple_of(h * half + u * part_rows, part_rows), part_rows)

    def shares(e):
        return pl.ds(pl.multiple_of(e * share, share), share)

    def blocks(i):
        return pl.ds(pl.multiple_of(i * BLOCK, BLOCK), BLOCK)

    def chunks(q):
        return pl.ds(pl.multiple_of(q * chunk, chunk), chunk)

    def weights(k):
        return (
            pltpu.make_async_copy(w_gate.at[:, blocks(k)], w_in.at[k, 0], w_s.at[k, 0]),
            pltpu.make_async_copy(w_up.at[:, blocks(k)], w_in.at[k, 1], w_s.at[k, 1]),
            pltpu.make_async_copy(w_down.at[blocks(k), :], w_dn.at[k], w_s.at[k, 2]),
        )

    def own_copy(a):
        src, dst = ((tok, x), (cot, dy))[a]
        return pltpu.make_async_copy(src, dst.at[0, shares(core), :], own_s.at[a])

    masks = [
        pltpu.make_async_copy(mask_in, keep_in, keep_s.at[0]),
        pltpu.make_async_copy(mask_out, keep_out, keep_s.at[1]),
    ]
    for copy in masks:
        copy.start()
    for copy in weights(0):
        copy.start()
    for a in range(2):
        own_copy(a).start()

    barrier = pltpu.get_barrier_semaphore()
    pl.semaphore_signal(barrier, inc=1, device_id=(inner, c), device_id_type=MESH)
    pl.semaphore_signal(barrier, inc=1, device_id=sibling, device_id_type=MESH)
    for q in range(1, chips):
        pl.semaphore_signal(barrier, inc=1, device_id=partner(q), device_id_type=MESH)

    @pl.when(has_outer)
    def _():
        pl.semaphore_signal(barrier, inc=1, device_id=(outer, c), device_id_type=MESH)

    def prepare(k):
        for copy in weights(k):
            copy.wait()

        @pl.loop(0, pieces)
        def _(i):
            at = blocks(i)
            keep = keep_in[k, i].astype(F32)
            w_in[k, 0, at, :] = (w_in[k, 0, at, :].astype(F32) * keep).astype(BF16)
            w_in[k, 1, at, :] = (w_in[k, 1, at, :].astype(F32) * keep).astype(BF16)
            w_dn[k, :, at] = (w_dn[k, :, at].astype(F32) * keep_out[k, i].astype(F32)).astype(BF16)

    for copy in masks:
        copy.wait()
    prepare(0)
    pl.semaphore_wait(barrier, jnp.where(has_outer, chips + 2, chips + 1))

    def to_sibling(a):
        src, dst = ((tok, x), (cot, dy))[a]
        return pltpu.make_async_remote_copy(
            src_ref=src, dst_ref=dst.at[0, shares(core), :], send_sem=sib_ss.at[a],
            recv_sem=sib_rs.at[a], device_id=sibling, device_id_type=MESH,
        )

    def to_chip(a, q):
        src, dst = ((tok, x), (cot, dy))[a]
        return pltpu.make_async_remote_copy(
            src_ref=src, dst_ref=dst.at[q, shares(core), :], send_sem=ag_ss.at[a, q - 1],
            recv_sem=ag_rs.at[a, q - 1], device_id=partner(q), device_id_type=MESH,
        )

    def forward(a, q):
        ref = (x, dy)[a].at[q, shares(core), :]
        return pltpu.make_async_remote_copy(
            src_ref=ref, dst_ref=ref, send_sem=fw_ss.at[a, q - 1],
            recv_sem=fw_rs.at[a, q - 1], device_id=sibling, device_id_type=MESH,
        )

    for a in range(2):
        to_sibling(a).start()
    if units > 1:
        for copy in weights(1):
            copy.start()

    def send_inner(t, h, u):
        ref = part.at[t, :, rows_of(h, u), :]
        return pltpu.make_async_remote_copy(
            src_ref=ref, dst_ref=ref, send_sem=p_ss.at[t, h, u],
            recv_sem=a_rs.at[t, h, u], device_id=(inner, c), device_id_type=MESH,
        )

    def send_middle(t, u):
        return pltpu.make_async_remote_copy(
            src_ref=part.at[t, :, rows_of(given, u), :], dst_ref=other.at[t, :, rows_of(0, u), :],
            send_sem=p_ss.at[t, given, u], recv_sem=b_rs.at[t, u], device_id=(inner, c), device_id_type=MESH,
        )

    def share_inner(t, h, u):
        ref = fin.at[t, :, rows_of(h, u), :]
        return pltpu.make_async_remote_copy(
            src_ref=ref, dst_ref=ref, send_sem=fi_ss.at[t, u],
            recv_sem=f_rs.at[t, h, u], device_id=(inner, c), device_id_type=MESH,
        )

    def share_outer(t, h, u):
        ref = fin.at[t, :, rows_of(h, u), :]
        return pltpu.make_async_remote_copy(
            src_ref=ref, dst_ref=ref, send_sem=fo_ss.at[t, h, u],
            recv_sem=f_rs.at[t, h, u], device_id=(outer, c), device_id_type=MESH,
        )

    def save_xt(q):
        if not turn:
            return pltpu.make_async_copy(x.at[q], xt_out.at[chunks(q), :], xt_s.at[q])
        return pltpu.make_async_copy(xt.at[lax.rem(q, 2)], xt_out.at[:, chunks(q)], xt_s.at[q])

    def save_dy(q):
        return pltpu.make_async_copy(dy.at[q], dy_out.at[chunks(q), :], dy_s.at[q])

    def save_fin(t):
        q, k = lax.div(t, units), lax.rem(t, units)
        return pltpu.make_async_copy(
            fin.at[t, pl.ds(0, 2)], fin_out.at[:, chunks(q), blocks(k)], fin_s.at[t]
        )

    def save_ht(t):
        q, k = lax.div(t, units), lax.rem(t, units)
        if not turn:
            return pltpu.make_async_copy(fin.at[t, 2], ht_out.at[chunks(q), blocks(k)], ht_s.at[t])
        return pltpu.make_async_copy(ht.at[t], ht_out.at[blocks(k), chunks(q)], ht_s.at[t])

    def produce(t):
        q, k = lax.div(t, units), lax.rem(t, units)
        s = lax.rem(t, OWN_SLOTS)

        @pl.when(t == 0)
        def _():
            own_copy(0).wait()
            to_sibling(0).wait_recv()

        @pl.when((k == 0) & (q > 0))
        def _():
            for a in range(2):
                forward(a, q).wait_recv()

        @pl.when(t + 2 < units)
        def _():
            for copy in weights(t + 2):
                copy.start()

        @pl.when((q == 0) & (k > 0))
        def _():
            prepare(k)

        own[s, 0] = dot(x[q], w_in[k, 0], ((1,), (0,)))
        own[s, 1] = dot(x[q], w_in[k, 1], ((1,), (0,)))

        @pl.when(t == 0)
        def _():
            own_copy(1).wait()
            to_sibling(1).wait_recv()

        own[s, 2] = dot(dy[q], w_dn[k], ((1,), (1,)))

    def reduce(t):
        s = lax.rem(t, OWN_SLOTS)

        def rounded(h, u):
            at = rows_of(h, u)

            @pl.when(has_outer)
            def _():
                send_inner(t, h, u).wait_recv()
                for j in range(3):
                    part[t, j, at, :] = (own[s, j, at, :] + part[t, j, at, :].astype(F32)).astype(BF16)

            @pl.when(jnp.logical_not(has_outer))
            def _():
                for j in range(3):
                    part[t, j, at, :] = own[s, j, at, :].astype(BF16)

        @pl.loop(0, split)
        def _(u):
            rounded(given, u)

            @pl.when(middle)
            def _():
                send_middle(t, u).start()

            @pl.when(jnp.logical_not(middle))
            def _():
                send_inner(t, given, u).start()

        @pl.when(jnp.logical_not(middle))
        def _():
            @pl.loop(0, split)
            def _(u):
                rounded(owned, u)
                send_inner(t, owned, u).start()

    def finish(t):
        s = lax.rem(t, OWN_SLOTS)

        def one(u):
            at = rows_of(owned, u)
            there = rows_of(0, u)

            @pl.when(has_outer)
            def _():
                send_inner(t, owned, u).wait_recv()
                for j in range(3):
                    own[s, j, at, :] += part[t, j, at, :].astype(F32)

            send_middle(t, u).wait_recv()
            gate = own[s, 0, at, :] + other[t, 0, there, :].astype(F32)
            up = own[s, 1, at, :] + other[t, 1, there, :].astype(F32)
            grad = own[s, 2, at, :] + other[t, 2, there, :].astype(F32)
            sig = jax.nn.sigmoid(gate)
            act = gate * sig
            fin[t, 0, at, :] = (grad * up * sig * (1.0 + gate * (1.0 - sig))).astype(BF16)
            fin[t, 1, at, :] = (grad * act).astype(BF16)
            fin[t, 2, at, :] = (act * up).astype(BF16)

            share_inner(t, owned, u).start()

            @pl.when(has_outer)
            def _():
                share_outer(t, owned, u).start()

        @pl.when(middle)
        def _():
            pl.loop(0, split)(one)

    def arrived(t):
        def one(h, u):
            share_inner(t, h, u).wait_recv()

            @pl.when(has_outer)
            def _():
                share_outer(t, h, u).start()

        @pl.loop(0, split)
        def _(u):
            one(given, u)

            @pl.when(jnp.logical_not(middle))
            def _():
                one(owned, u)

    def transpose_tokens(t):
        q, k = lax.div(t, units), lax.rem(t, units)

        if turn:
            @pl.when((k == 0) & (q >= 2))
            def _():
                save_xt(q - 2).wait()

            @pl.loop(lax.div(k * pieces, units), lax.div((k + 1) * pieces, units))
            def _(i):
                xt[lax.rem(q, 2), blocks(i), :] = x[q, :, blocks(i)].T

        @pl.when(k == units - 1)
        def _():
            save_xt(q).start()
            save_dy(q).start()

        @pl.when((k == max(0, units - 2)) & (q + 1 < chips))
        def _():
            for a in range(2):
                to_chip(a, q + 1).wait_recv()
                forward(a, q + 1).start()

    def to_sibling_sum(q, a):
        return pltpu.make_async_remote_copy(
            src_ref=acc.at[lax.rem(q, 2), a, shares(1 - core), :], dst_ref=sib.at[q, a],
            send_sem=rx_ss.at[q, a], recv_sem=rx_rs.at[q, a], device_id=sibling, device_id_type=MESH,
        )

    def scatter(q):
        return pltpu.make_async_remote_copy(
            src_ref=rs_send.at[q - 1], dst_ref=rs_recv.at[q - 1], send_sem=rs_ss.at[q - 1],
            recv_sem=rs_rs.at[q - 1], device_id=partner(q), device_id_type=MESH,
        )

    def consume(t):
        q, k = lax.div(t, units), lax.rem(t, units)
        b = lax.rem(q, 2)

        @pl.when(k == 0)
        def _():
            acc[b] = jnp.zeros_like(acc[b])

        save_fin(t).start()
        acc[b, 0] += dot(fin[t, 2], w_dn[k], ((1,), (0,)))

        @pl.when(k == units - 1)
        def _():
            to_sibling_sum(q, 0).start()

        acc[b, 1] += dot(fin[t, 0], w_in[k, 0], ((1,), (1,))) + dot(
            fin[t, 1], w_in[k, 1], ((1,), (1,))
        )

        @pl.when(k == units - 1)
        def _():
            to_sibling_sum(q, 1).start()

        if turn:
            ht[t] = fin[t, 2].T
        save_ht(t).start()

    def sent(t):
        @pl.loop(0, split)
        def _(u):
            @pl.when(middle)
            def _():
                send_middle(t, u).wait_send()
                share_inner(t, owned, u).wait_send()

            @pl.when(jnp.logical_not(middle))
            def _():
                for h in range(2):
                    send_inner(t, h, u).wait_send()

            @pl.when(has_outer)
            def _():
                for h in range(2):
                    share_outer(t, h, u).wait_send()

    def saved(t):
        save_fin(t).wait()
        save_ht(t).wait()

    def gathered():
        for a in range(2):
            to_sibling(a).wait_send()
            for q in range(1, chips):
                to_chip(a, q).wait_send()
                forward(a, q).wait_send()
        for q in range(last):
            save_dy(q).wait()
            if q < last - 1 and turn:
                continue
            save_xt(q).wait()

    def settle(q):
        at = shares(core)
        for a in range(2):
            to_sibling_sum(q, a).wait()
            sib[q, a] += acc[lax.rem(q, 2), a, at, :]

    @pl.loop(0, count + LAG_USE)
    def _(t):
        @pl.when(t < count)
        def _():
            produce(t)
            reduce(t)

        @pl.when(t == 0)
        def _():
            for q in range(1, chips):
                for a in range(2):
                    to_chip(a, q).start()

        @pl.when((t >= LAG_OWN) & (t < count + LAG_OWN))
        def _():
            finish(t - LAG_OWN)

        @pl.when(has_outer & (t >= LAG_FWD) & (t < count + LAG_FWD))
        def _():
            arrived(t - LAG_FWD)

        @pl.when(t < count)
        def _():
            transpose_tokens(t)

        @pl.when((t >= KEPT) & (t < count + KEPT))
        def _():
            sent(t - KEPT)

        @pl.when(t == count - 1)
        def _():
            gathered()

        @pl.when(t >= LAG_USE)
        def _():
            u = t - LAG_USE

            @pl.when(jnp.logical_not(has_outer))
            def _():
                arrived(u)

            consume(u)

            @pl.when(u >= SAVED)
            def _():
                saved(u - SAVED)

            q = lax.div(u, units) - 1

            @pl.when((lax.rem(u, units) == 1) & (q >= 0))
            def _():
                settle(q)

                @pl.when(q > 0)
                def _():
                    for a in range(2):
                        rs_send[q - 1, a] = sib[q, a].astype(BF16)
                    scatter(q).start()

    for q in range(1, last):
        scatter(q).wait()
        for a in range(2):
            sib[0, a] += rs_recv[q - 1, a].astype(F32)
    save_base = pltpu.make_async_copy(sib.at[0], base, end_s.at[0])
    save_base.start()
    for a in range(2):
        to_sibling_sum(last, a).wait()
        rs_send[last - 1, a] = (sib[last, a] + acc[last % 2, a, shares(core), :]).astype(BF16)
    save_tail = pltpu.make_async_copy(rs_send.at[last - 1], tail, end_s.at[1])
    save_tail.start()

    @pl.loop(max(0, count - SAVED), count)
    def _(t):
        saved(t)

    @pl.loop(max(0, count + LAG_USE - KEPT), count)
    def _(t):
        sent(t)

    save_dy(last).wait()
    save_xt(last).wait()
    save_base.wait()
    save_tail.wait()


def wgrad_kernel(
    xt_in, dy_in, fin_in, ht_in, mask_in, mask_out, gate_w, up_w, down_w,
    xt, ht, fin, dy, gate_o, up_o, down_o, order, keep_in, keep_out, keep_s, xt_s, ht_s, fin_s, dy_s, gate_s, up_s, down_s,
):
    pieces = xt.shape[0] // BLOCK
    units = ht.shape[0] // BLOCK

    def blocks(i):
        return pl.ds(pl.multiple_of(i * BLOCK, BLOCK), BLOCK)

    def load_fin(k):
        return pltpu.make_async_copy(fin_in.at[:, :, blocks(k)], fin.at[k], fin_s.at[k])

    def load_dy(i):
        return pltpu.make_async_copy(dy_in.at[:, blocks(i)], dy.at[i], dy_s.at[i])

    def saves(k):
        b = lax.rem(k, 2)
        return (
            pltpu.make_async_copy(gate_o.at[b], gate_w.at[:, blocks(k)], gate_s.at[b]),
            pltpu.make_async_copy(up_o.at[b], up_w.at[:, blocks(k)], up_s.at[b]),
        )

    def save_down(i):
        b = lax.rem(i, 2)
        return pltpu.make_async_copy(down_o.at[b], down_w.at[:, blocks(i)], down_s.at[b])

    masks = [
        pltpu.make_async_copy(mask_in, keep_in, keep_s.at[0]),
        pltpu.make_async_copy(mask_out, keep_out, keep_s.at[1]),
    ]
    load_xt = pltpu.make_async_copy(xt_in, xt, xt_s)
    load_ht = pltpu.make_async_copy(ht_in, ht, ht_s)
    load_fin(0).start()
    load_xt.start()
    for copy in masks:
        copy.start()
    load_dy(0).start()
    load_ht.start()

    @pl.loop(1, units)
    def _(k):
        load_fin(k).start()

    @pl.loop(1, pieces)
    def _(i):
        load_dy(i).start()

    def sort(kind, column, length, kept):
        def put(i, n):
            keep = kept(i)
            order[kind, column, jnp.where(keep != 0, n, length - 1 - (i - n))] = i
            return n + keep

        order[kind, column, length] = lax.fori_loop(0, length, put, 0)

    for copy in masks:
        copy.wait()

    @pl.loop(0, units)
    def _(k):
        sort(0, k, pieces, lambda i: keep_in[k, i])

    @pl.loop(0, pieces)
    def _(i):
        sort(1, i, units, lambda k: keep_out[k, i])

    def products(kind, column, length, left, pairs, kept):
        kept_count = order[kind, column, length]
        step = max(1, length // 8)
        for size in range(step, length + 1, step):
            lowest = kept_count > size - step if size > step else kept_count >= 0

            @pl.when(lowest & (kept_count <= size))
            def _():
                places = [order[kind, column, n] for n in range(length)]
                rows = jnp.concatenate([left[blocks(places[n]), :] for n in range(size)], axis=0)
                for right, out in pairs:
                    whole = dot(rows, right, ((1,), (0,)))
                    for n in range(size):
                        piece = whole[n * BLOCK : (n + 1) * BLOCK]
                        if n >= size - step:
                            piece = piece * kept(places[n]).astype(F32)
                        out[blocks(places[n]), :] = piece.astype(BF16)
                    for n in range(size, length):
                        out[blocks(places[n]), :] = jnp.zeros((BLOCK, BLOCK), BF16)

    def inward(k):
        b = lax.rem(k, 2)
        load_fin(k).wait()

        @pl.when(k >= 2)
        def _():
            for copy in saves(k - 2):
                copy.wait()

        products(
            0, k, pieces, xt, ((fin[k, 0], gate_o.at[b]), (fin[k, 1], up_o.at[b])),
            lambda i: keep_in[k, i],
        )
        for copy in saves(k):
            copy.start()

    def outward(i):
        b = lax.rem(i, 2)
        load_dy(i).wait()

        @pl.when(i >= 2)
        def _():
            save_down(i - 2).wait()

        products(1, i, units, ht, ((dy[i], down_o.at[b]),), lambda k: keep_out[k, i])
        save_down(i).start()

    load_xt.wait()

    @pl.loop(0, max(units, pieces))
    def _(n):
        @pl.when(n < units)
        def _():
            inward(n)

        @pl.when(n == 0)
        def _():
            load_ht.wait()

        @pl.when(n < pieces)
        def _():
            outward(n)

    for k in range(max(0, units - 2), units):
        for copy in saves(k):
            copy.wait()
    for i in range(max(0, pieces - 2), pieces):
        save_down(i).wait()


def weight_grads(xt, dy, fin, ht, mask_in, mask_out):
    width, total = xt.shape
    hidden = ht.shape[0]
    pieces, units = width // BLOCK, hidden // BLOCK
    struct = jax.ShapeDtypeStruct
    anywhere = pl.BlockSpec(memory_space=pl.ANY)
    dma = pltpu.SemaphoreType.DMA
    return pl.pallas_call(
        wgrad_kernel,
        out_shape=(
            struct((width, hidden), BF16),
            struct((width, hidden), BF16),
            struct((hidden, width), BF16),
        ),
        in_specs=[anywhere] * 6,
        out_specs=(anywhere,) * 3,
        scratch_shapes=[
            pltpu.VMEM((width, total), BF16),
            pltpu.VMEM((hidden, total), BF16),
            pltpu.VMEM((units, 2, total, BLOCK), BF16),
            pltpu.VMEM((pieces, total, BLOCK), BF16),
            pltpu.VMEM((2, width, BLOCK), BF16),
            pltpu.VMEM((2, width, BLOCK), BF16),
            pltpu.VMEM((2, hidden, BLOCK), BF16),
            pltpu.SMEM((2, max(units, pieces), max(units, pieces) + 1), jnp.int32),
            pltpu.SMEM((units, pieces), jnp.int32),
            pltpu.SMEM((units, pieces), jnp.int32),
            dma((2,)),
            dma, dma, dma((units,)), dma((pieces,)), dma((2,)), dma((2,)), dma((2,)),
        ],
        compiler_params=pltpu.CompilerParams(vmem_limit_bytes=60 * 1024 * 1024),
        cost_estimate=pl.CostEstimate(
            flops=6 * total * width * hidden,
            bytes_accessed=6 * width * hidden + 10 * total * width,
            transcendentals=0,
        ),
        name="wgrad",
    )(xt, dy, fin, ht, mask_in, mask_out)


def local(rows, cols, tokens, w_gate, w_up, w_down, mask_in, mask_out, out_grad):
    share, width = tokens.shape
    hidden = w_gate.shape[1]
    units = hidden // BLOCK
    total = share * cols
    chips = cols // CORES
    chunk = CORES * share
    count = chips * units
    anywhere = pl.BlockSpec(memory_space=pl.ANY)
    dma = pltpu.SemaphoreType.DMA
    struct = jax.ShapeDtypeStruct
    base, tail, xt, dy, fin, ht = pl.pallas_call(
        functools.partial(step_kernel, rows, cols, units),
        out_shape=(
            struct((2, share, width), F32),
            struct((2, share, width), BF16),
            struct((width, total) if turned(chunk) else (total, width), BF16),
            struct((total, width), BF16),
            struct((2, total, hidden), BF16),
            struct((hidden, total) if turned(chunk) else (total, hidden), BF16),
        ),
        in_specs=[anywhere] * 7,
        out_specs=(anywhere,) * 6,
        scratch_shapes=[
            pltpu.VMEM((chips, chunk, width), BF16),
            pltpu.VMEM((chips, chunk, width), BF16),
            pltpu.VMEM((2, width, chunk), BF16),
            pltpu.VMEM((count, 3, chunk, BLOCK), BF16),
            pltpu.VMEM((count, 3, chunk // 2, BLOCK), BF16),
            pltpu.VMEM((count, 3, chunk, BLOCK), BF16),
            pltpu.VMEM((count, BLOCK, chunk) if turned(chunk) else (1, 16, 128), BF16),
            pltpu.VMEM((OWN_SLOTS, 3, chunk, BLOCK), F32),
            pltpu.VMEM((units, 2, width, BLOCK), BF16),
            pltpu.VMEM((units, BLOCK, width), BF16),
            pltpu.VMEM((2, 2, chunk, width), F32),
            pltpu.VMEM((chips, 2, share, width), F32),
            pltpu.VMEM((chips - 1, 2, share, width), BF16),
            pltpu.VMEM((chips - 2, 2, share, width), BF16),
            pltpu.SMEM((units, width // BLOCK), jnp.int32),
            pltpu.SMEM((units, width // BLOCK), jnp.int32),
            dma((2,)),
            dma((2,)), dma((2,)), dma((2,)),
            dma((2, chips - 1)), dma((2, chips - 1)),
            dma((2, chips - 1)), dma((2, chips - 1)),
            dma((units, 3)),
            dma((count, 2, SPLIT)), dma((count, 2, SPLIT)), dma((count, SPLIT)),
            dma((count, SPLIT)), dma((count, 2, SPLIT)), dma((count, 2, SPLIT)),
            dma((chips,)), dma((chips,)), dma((count,)), dma((count,)),
            dma((chips, 2)), dma((chips, 2)),
            dma((chips - 2,)), dma((chips - 2,)),
            dma((2,)),
        ],
        compiler_params=pltpu.CompilerParams(
            collective_id=0, has_side_effects=True, vmem_limit_bytes=63 * 1024 * 1024
        ),
        cost_estimate=pl.CostEstimate(
            flops=12 * total * width * hidden,
            bytes_accessed=6 * width * hidden,
            transcendentals=total * hidden,
        ),
        name="step",
    )(tokens, out_grad, w_gate, w_up, w_down, mask_in, mask_out)
    if not turned(chunk):
        xt, ht = xt.T, ht.T
    nearest = [(i, (i // CORES ^ 1) * CORES + i % CORES) for i in range(cols)]
    moved = lax.ppermute(tail, "col", nearest)
    gate_wgrad, up_wgrad, down_wgrad = weight_grads(xt, dy, fin, ht, mask_in, mask_out)
    output, tokens_grad = [(base[a] + moved[a].astype(F32)).astype(BF16) for a in range(2)]
    return output, tokens_grad, gate_wgrad, up_wgrad, down_wgrad


def solution(mesh):
    placed = (
        P("col", "row"),
        P("row", "col"),
        P("row", "col"),
        P("col", "row"),
        P("col", "row"),
        P("col", "row"),
        P("col", "row"),
    )
    return jax.shard_map(
        functools.partial(local, mesh.shape["row"], mesh.shape["col"]),
        mesh=mesh,
        in_specs=placed,
        out_specs=(
            P("col", "row"),
            P("col", "row"),
            P("row", "col"),
            P("row", "col"),
            P("col", "row"),
        ),
        check_vma=False,
    )
```

```python
import functools

import jax
import jax.numpy as jnp
from jax import lax
from jax.experimental import pallas as pl
from jax.experimental.pallas import tpu as pltpu
from jax.sharding import PartitionSpec as P

BLOCK = 256
CORES = 2
LAG_OWN = 1
LAG_FWD = 2
LAG_USE = 5
OWN_SLOTS = LAG_OWN + 1
KEPT = 10
SAVED = 3
SPLIT = 1
MESH = pl.DeviceIdType.MESH
F32 = jnp.float32
BF16 = jnp.bfloat16


def dot(left, right, dims):
    return lax.dot_general(left, right, (dims, ((), ())), preferred_element_type=F32)


def turned(chunk):
    return chunk % 128 == 0


def flip(chip, j, chips):
    other, bit = chip, 1
    while bit < chips:
        other = other + lax.rem(lax.div(j, bit), 2) * (bit - 2 * bit * lax.rem(lax.div(chip, bit), 2))
        bit *= 2
    return other


def place(q, chips):
    return jnp.where(q == 0, 0, jnp.where(q == chips - 1, 1, q + 1))


def step_kernel(
    rows, cols, units,
    tok, cot, w_gate, w_up, w_down, mask_in, mask_out,
    base, tail, xt_out, dy_out, fin_out, ht_out,
    x, dy, xt, part, other, fin, ht, own, w_in, w_dn, acc, sib, rs_send, rs_recv,
    keep_in, keep_out, keep_s,
    own_s, sib_ss, sib_rs, ag_ss, ag_rs, fw_ss, fw_rs, w_s, p_ss, a_rs, b_rs, fi_ss, fo_ss, f_rs,
    xt_s, dy_s, fin_s, ht_s, rx_ss, rx_rs, rs_ss, rs_rs, end_s,
):
    r = lax.axis_index("row")
    c = lax.axis_index("col")
    chips = cols // CORES
    chip, core = lax.div(c, CORES), lax.rem(c, CORES)
    low = r < rows // 2
    inner = jnp.where(low, r + 1, r - 1)
    outer = jnp.where(low, r - 1, r + 1)
    has_outer = (r > 0) & (r < rows - 1)
    middle = (r == rows // 2 - 1) | (r == rows // 2)
    outermost = jnp.logical_not(has_outer | middle)
    owned = jnp.where(low, 0, 1)
    given = 1 - owned
    share, width = tok.shape
    chunk = CORES * share
    half = chunk // 2
    split = SPLIT
    part_rows = half // split
    pieces = width // BLOCK
    count = chips * units
    last = chips - 1
    turn = turned(chunk)
    sibling = (r, chip * CORES + (1 - core))

    def partner(q):
        return (r, flip(chip, place(q, chips), chips) * CORES + core)

    def rows_of(h, u):
        return pl.ds(pl.multiple_of(h * half + u * part_rows, part_rows), part_rows)

    def shares(e):
        return pl.ds(pl.multiple_of(e * share, share), share)

    def blocks(i):
        return pl.ds(pl.multiple_of(i * BLOCK, BLOCK), BLOCK)

    def chunks(q):
        return pl.ds(pl.multiple_of(q * chunk, chunk), chunk)

    def weights(k):
        return (
            pltpu.make_async_copy(w_gate.at[:, blocks(k)], w_in.at[k, 0], w_s.at[k, 0]),
            pltpu.make_async_copy(w_up.at[:, blocks(k)], w_in.at[k, 1], w_s.at[k, 1]),
            pltpu.make_async_copy(w_down.at[blocks(k), :], w_dn.at[k], w_s.at[k, 2]),
        )

    def own_copy(a):
        src, dst = ((tok, x), (cot, dy))[a]
        return pltpu.make_async_copy(src, dst.at[0, shares(core), :], own_s.at[a])

    masks = [
        pltpu.make_async_copy(mask_in, keep_in, keep_s.at[0]),
        pltpu.make_async_copy(mask_out, keep_out, keep_s.at[1]),
    ]
    for copy in masks:
        copy.start()
    for copy in weights(0):
        copy.start()
    for a in range(2):
        own_copy(a).start()

    barrier = pltpu.get_barrier_semaphore()
    pl.semaphore_signal(barrier, inc=1, device_id=(inner, c), device_id_type=MESH)
    pl.semaphore_signal(barrier, inc=1, device_id=sibling, device_id_type=MESH)
    for q in range(1, chips):
        pl.semaphore_signal(barrier, inc=1, device_id=partner(q), device_id_type=MESH)

    @pl.when(has_outer)
    def _():
        pl.semaphore_signal(barrier, inc=1, device_id=(outer, c), device_id_type=MESH)

    def prepare(k):
        for copy in weights(k):
            copy.wait()

        @pl.loop(0, pieces)
        def _(i):
            at = blocks(i)
            keep = keep_in[k, i].astype(F32)
            w_in[k, 0, at, :] = (w_in[k, 0, at, :].astype(F32) * keep).astype(BF16)
            w_in[k, 1, at, :] = (w_in[k, 1, at, :].astype(F32) * keep).astype(BF16)
            w_dn[k, :, at] = (w_dn[k, :, at].astype(F32) * keep_out[k, i].astype(F32)).astype(BF16)

    for copy in masks:
        copy.wait()
    prepare(0)

    def first_half(e, arrays):
        at = shares(e)
        for j in arrays:
            if j < 2:
                own[0, j, at, :] = dot(x[0, at, :], w_in[0, j], ((1,), (0,)))
            else:
                own[0, j, at, :] = dot(dy[0, at, :], w_dn[0], ((1,), (1,)))

    for a in range(2):
        own_copy(a).wait()
    first_half(core, (0, 1, 2))
    pl.semaphore_wait(barrier, jnp.where(has_outer, chips + 2, chips + 1))

    def to_sibling(a):
        src, dst = ((tok, x), (cot, dy))[a]
        return pltpu.make_async_remote_copy(
            src_ref=src, dst_ref=dst.at[0, shares(core), :], send_sem=sib_ss.at[a],
            recv_sem=sib_rs.at[a], device_id=sibling, device_id_type=MESH,
        )

    def to_chip(a, q):
        src, dst = ((tok, x), (cot, dy))[a]
        return pltpu.make_async_remote_copy(
            src_ref=src, dst_ref=dst.at[q, shares(core), :], send_sem=ag_ss.at[a, q - 1],
            recv_sem=ag_rs.at[a, q - 1], device_id=partner(q), device_id_type=MESH,
        )

    def forward(a, q):
        ref = (x, dy)[a].at[q, shares(core), :]
        return pltpu.make_async_remote_copy(
            src_ref=ref, dst_ref=ref, send_sem=fw_ss.at[a, q - 1],
            recv_sem=fw_rs.at[a, q - 1], device_id=sibling, device_id_type=MESH,
        )

    for a in range(2):
        to_sibling(a).start()
    if units > 1:
        for copy in weights(1):
            copy.start()

    def send_inner(t, h, u):
        ref = part.at[t, :, rows_of(h, u), :]
        return pltpu.make_async_remote_copy(
            src_ref=ref, dst_ref=ref, send_sem=p_ss.at[t, h, u],
            recv_sem=a_rs.at[t, h, u], device_id=(inner, c), device_id_type=MESH,
        )

    def send_middle(t, u):
        return pltpu.make_async_remote_copy(
            src_ref=part.at[t, :, rows_of(given, u), :], dst_ref=other.at[t, :, rows_of(0, u), :],
            send_sem=p_ss.at[t, given, u], recv_sem=b_rs.at[t, u], device_id=(inner, c), device_id_type=MESH,
        )

    def share_inner(t, h, u):
        ref = fin.at[t, :, rows_of(h, u), :]
        return pltpu.make_async_remote_copy(
            src_ref=ref, dst_ref=ref, send_sem=fi_ss.at[t, u],
            recv_sem=f_rs.at[t, h, u], device_id=(inner, c), device_id_type=MESH,
        )

    def share_outer(t, h, u):
        ref = fin.at[t, :, rows_of(h, u), :]
        return pltpu.make_async_remote_copy(
            src_ref=ref, dst_ref=ref, send_sem=fo_ss.at[t, h, u],
            recv_sem=f_rs.at[t, h, u], device_id=(outer, c), device_id_type=MESH,
        )

    def save_xt(q):
        if not turn:
            return pltpu.make_async_copy(x.at[q], xt_out.at[chunks(q), :], xt_s.at[q])
        return pltpu.make_async_copy(xt.at[lax.rem(q, 2)], xt_out.at[:, chunks(q)], xt_s.at[q])

    def save_dy(q):
        return pltpu.make_async_copy(dy.at[q], dy_out.at[chunks(q), :], dy_s.at[q])

    def save_fin(t):
        q, k = lax.div(t, units), lax.rem(t, units)
        return pltpu.make_async_copy(
            fin.at[t, pl.ds(0, 2)], fin_out.at[:, chunks(q), blocks(k)], fin_s.at[t]
        )

    def save_ht(t):
        q, k = lax.div(t, units), lax.rem(t, units)
        if not turn:
            return pltpu.make_async_copy(fin.at[t, 2], ht_out.at[chunks(q), blocks(k)], ht_s.at[t])
        return pltpu.make_async_copy(ht.at[t], ht_out.at[blocks(k), chunks(q)], ht_s.at[t])

    def produce(t):
        q, k = lax.div(t, units), lax.rem(t, units)
        s = lax.rem(t, OWN_SLOTS)

        @pl.when((k == 0) & (q > 0))
        def _():
            for a in range(2):
                forward(a, q).wait_recv()

        @pl.when(t + 2 < units)
        def _():
            for copy in weights(t + 2):
                copy.start()

        @pl.when((q == 0) & (k > 0))
        def _():
            prepare(k)

        @pl.when(t == 0)
        def _():
            to_sibling(0).wait_recv()
            first_half(1 - core, (0, 1))
            to_sibling(1).wait_recv()
            first_half(1 - core, (2,))

        @pl.when(t > 0)
        def _():
            own[s, 0] = dot(x[q], w_in[k, 0], ((1,), (0,)))
            own[s, 1] = dot(x[q], w_in[k, 1], ((1,), (0,)))
            own[s, 2] = dot(dy[q], w_dn[k], ((1,), (1,)))

    def reduce(t):
        s = lax.rem(t, OWN_SLOTS)

        def rounded(h, u):
            at = rows_of(h, u)

            @pl.when(has_outer)
            def _():
                send_inner(t, h, u).wait_recv()
                for j in range(3):
                    part[t, j, at, :] = (own[s, j, at, :] + part[t, j, at, :].astype(F32)).astype(BF16)

            @pl.when(jnp.logical_not(has_outer))
            def _():
                for j in range(3):
                    part[t, j, at, :] = own[s, j, at, :].astype(BF16)

        @pl.loop(0, split)
        def _(u):
            rounded(given, u)

            @pl.when(middle)
            def _():
                send_middle(t, u).start()

            @pl.when(jnp.logical_not(middle))
            def _():
                send_inner(t, given, u).start()

        @pl.when(jnp.logical_not(middle))
        def _():
            @pl.loop(0, split)
            def _(u):
                rounded(owned, u)
                send_inner(t, owned, u).start()

    def reduce_first():
        @pl.when(outermost)
        def _():
            at = shares(1 - core)
            for j in range(3):
                part[0, j, at, :] = own[0, j, at, :].astype(BF16)
            send_inner(0, 1 - core, 0).start()

        @pl.when(jnp.logical_not(outermost))
        def _():
            reduce(0)

    def send_first():
        at = shares(core)
        for j in range(3):
            part[0, j, at, :] = own[0, j, at, :].astype(BF16)
        send_inner(0, core, 0).start()

    def finish(t):
        s = lax.rem(t, OWN_SLOTS)

        def one(u):
            at = rows_of(owned, u)
            there = rows_of(0, u)

            @pl.when(has_outer)
            def _():
                send_inner(t, owned, u).wait_recv()
                for j in range(3):
                    own[s, j, at, :] += part[t, j, at, :].astype(F32)

            send_middle(t, u).wait_recv()
            gate = own[s, 0, at, :] + other[t, 0, there, :].astype(F32)
            up = own[s, 1, at, :] + other[t, 1, there, :].astype(F32)
            grad = own[s, 2, at, :] + other[t, 2, there, :].astype(F32)
            sig = jax.nn.sigmoid(gate)
            act = gate * sig
            fin[t, 0, at, :] = (grad * up * sig * (1.0 + gate * (1.0 - sig))).astype(BF16)
            fin[t, 1, at, :] = (grad * act).astype(BF16)
            fin[t, 2, at, :] = (act * up).astype(BF16)

            share_inner(t, owned, u).start()

            @pl.when(has_outer)
            def _():
                share_outer(t, owned, u).start()

        @pl.when(middle)
        def _():
            pl.loop(0, split)(one)

    def arrived(t):
        def one(h, u):
            share_inner(t, h, u).wait_recv()

            @pl.when(has_outer)
            def _():
                share_outer(t, h, u).start()

        @pl.loop(0, split)
        def _(u):
            one(given, u)

            @pl.when(jnp.logical_not(middle))
            def _():
                one(owned, u)

    def transpose_tokens(t):
        q, k = lax.div(t, units), lax.rem(t, units)

        if turn:
            @pl.when((k == 0) & (q >= 2))
            def _():
                save_xt(q - 2).wait()

            @pl.loop(lax.div(k * pieces, units), lax.div((k + 1) * pieces, units))
            def _(i):
                xt[lax.rem(q, 2), blocks(i), :] = x[q, :, blocks(i)].T

        @pl.when(k == units - 1)
        def _():
            save_xt(q).start()
            save_dy(q).start()

        @pl.when((k == max(0, units - 2)) & (q + 1 < chips))
        def _():
            for a in range(2):
                to_chip(a, q + 1).wait_recv()
                forward(a, q + 1).start()

    def to_sibling_sum(q, a):
        return pltpu.make_async_remote_copy(
            src_ref=acc.at[lax.rem(q, 2), a, shares(1 - core), :], dst_ref=sib.at[q, a],
            send_sem=rx_ss.at[q, a], recv_sem=rx_rs.at[q, a], device_id=sibling, device_id_type=MESH,
        )

    def scatter(q):
        return pltpu.make_async_remote_copy(
            src_ref=rs_send.at[q - 1], dst_ref=rs_recv.at[q - 1], send_sem=rs_ss.at[q - 1],
            recv_sem=rs_rs.at[q - 1], device_id=partner(q), device_id_type=MESH,
        )

    def consume(t):
        q, k = lax.div(t, units), lax.rem(t, units)
        b = lax.rem(q, 2)

        @pl.when(k == 0)
        def _():
            acc[b] = jnp.zeros_like(acc[b])

        save_fin(t).start()
        acc[b, 0] += dot(fin[t, 2], w_dn[k], ((1,), (0,)))

        @pl.when(k == units - 1)
        def _():
            to_sibling_sum(q, 0).start()

        acc[b, 1] += dot(fin[t, 0], w_in[k, 0], ((1,), (1,))) + dot(
            fin[t, 1], w_in[k, 1], ((1,), (1,))
        )

        @pl.when(k == units - 1)
        def _():
            to_sibling_sum(q, 1).start()

        if turn:
            ht[t] = fin[t, 2].T
        save_ht(t).start()

    def sent(t):
        @pl.loop(0, split)
        def _(u):
            @pl.when(middle)
            def _():
                send_middle(t, u).wait_send()
                share_inner(t, owned, u).wait_send()

            @pl.when(jnp.logical_not(middle))
            def _():
                for h in range(2):
                    send_inner(t, h, u).wait_send()

            @pl.when(has_outer)
            def _():
                for h in range(2):
                    share_outer(t, h, u).wait_send()

    def saved(t):
        save_fin(t).wait()
        save_ht(t).wait()

    def gathered():
        for a in range(2):
            to_sibling(a).wait_send()
            for q in range(1, chips):
                to_chip(a, q).wait_send()
                forward(a, q).wait_send()
        for q in range(last):
            save_dy(q).wait()
            if q < last - 1 and turn:
                continue
            save_xt(q).wait()

    def settle(q):
        at = shares(core)
        for a in range(2):
            to_sibling_sum(q, a).wait()
            sib[q, a] += acc[lax.rem(q, 2), a, at, :]

    @pl.when(outermost)
    def _():
        send_first()

    @pl.loop(0, count + LAG_USE)
    def _(t):
        @pl.when(t < count)
        def _():
            produce(t)

            @pl.when(t == 0)
            def _():
                reduce_first()

            @pl.when(t > 0)
            def _():
                reduce(t)

        @pl.when(t == 0)
        def _():
            for q in range(1, chips):
                for a in range(2):
                    to_chip(a, q).start()

        @pl.when((t >= LAG_OWN) & (t < count + LAG_OWN))
        def _():
            finish(t - LAG_OWN)

        @pl.when(has_outer & (t >= LAG_FWD) & (t < count + LAG_FWD))
        def _():
            arrived(t - LAG_FWD)

        @pl.when(t < count)
        def _():
            transpose_tokens(t)

        @pl.when((t >= KEPT) & (t < count + KEPT))
        def _():
            sent(t - KEPT)

        @pl.when(t == count - 1)
        def _():
            gathered()

        @pl.when(t >= LAG_USE)
        def _():
            u = t - LAG_USE

            @pl.when(jnp.logical_not(has_outer))
            def _():
                arrived(u)

            consume(u)

            @pl.when(u >= SAVED)
            def _():
                saved(u - SAVED)

            q = lax.div(u, units) - 1

            @pl.when((lax.rem(u, units) == 1) & (q >= 0))
            def _():
                settle(q)

                @pl.when(q > 0)
                def _():
                    for a in range(2):
                        rs_send[q - 1, a] = sib[q, a].astype(BF16)
                    scatter(q).start()

    for q in range(1, last):
        scatter(q).wait()
        for a in range(2):
            sib[0, a] += rs_recv[q - 1, a].astype(F32)
    save_base = pltpu.make_async_copy(sib.at[0], base, end_s.at[0])
    save_base.start()
    for a in range(2):
        to_sibling_sum(last, a).wait()
        rs_send[last - 1, a] = (sib[last, a] + acc[last % 2, a, shares(core), :]).astype(BF16)
    save_tail = pltpu.make_async_copy(rs_send.at[last - 1], tail, end_s.at[1])
    save_tail.start()

    @pl.loop(max(0, count - SAVED), count)
    def _(t):
        saved(t)

    @pl.loop(max(0, count + LAG_USE - KEPT), count)
    def _(t):
        sent(t)

    save_dy(last).wait()
    save_xt(last).wait()
    save_base.wait()
    save_tail.wait()


def wgrad_kernel(
    xt_in, dy_in, fin_in, ht_in, mask_in, mask_out, gate_w, up_w, down_w,
    xt, ht, fin, dy, gate_o, up_o, down_o, order, keep_in, keep_out, keep_s, xt_s, ht_s, fin_s, dy_s, gate_s, up_s, down_s,
):
    pieces = xt.shape[0] // BLOCK
    units = ht.shape[0] // BLOCK

    def blocks(i):
        return pl.ds(pl.multiple_of(i * BLOCK, BLOCK), BLOCK)

    def load_fin(k):
        return pltpu.make_async_copy(fin_in.at[:, :, blocks(k)], fin.at[k], fin_s.at[k])

    def load_dy(i):
        return pltpu.make_async_copy(dy_in.at[:, blocks(i)], dy.at[i], dy_s.at[i])

    def saves(k):
        b = lax.rem(k, 2)
        return (
            pltpu.make_async_copy(gate_o.at[b], gate_w.at[:, blocks(k)], gate_s.at[b]),
            pltpu.make_async_copy(up_o.at[b], up_w.at[:, blocks(k)], up_s.at[b]),
        )

    def save_down(i):
        b = lax.rem(i, 2)
        return pltpu.make_async_copy(down_o.at[b], down_w.at[:, blocks(i)], down_s.at[b])

    masks = [
        pltpu.make_async_copy(mask_in, keep_in, keep_s.at[0]),
        pltpu.make_async_copy(mask_out, keep_out, keep_s.at[1]),
    ]
    load_xt = pltpu.make_async_copy(xt_in, xt, xt_s)
    load_ht = pltpu.make_async_copy(ht_in, ht, ht_s)
    load_fin(0).start()
    load_xt.start()
    for copy in masks:
        copy.start()
    load_dy(0).start()
    load_ht.start()

    @pl.loop(1, units)
    def _(k):
        load_fin(k).start()

    @pl.loop(1, pieces)
    def _(i):
        load_dy(i).start()

    def sort(kind, column, length, kept):
        def put(i, n):
            keep = kept(i)
            order[kind, column, jnp.where(keep != 0, n, length - 1 - (i - n))] = i
            return n + keep

        order[kind, column, length] = lax.fori_loop(0, length, put, 0)

    for copy in masks:
        copy.wait()

    @pl.loop(0, units)
    def _(k):
        sort(0, k, pieces, lambda i: keep_in[k, i])

    @pl.loop(0, pieces)
    def _(i):
        sort(1, i, units, lambda k: keep_out[k, i])

    def products(kind, column, length, left, pairs, kept):
        kept_count = order[kind, column, length]
        step = max(1, length // 8)
        for size in range(step, length + 1, step):
            lowest = kept_count > size - step if size > step else kept_count >= 0

            @pl.when(lowest & (kept_count <= size))
            def _():
                places = [order[kind, column, n] for n in range(length)]
                rows = jnp.concatenate([left[blocks(places[n]), :] for n in range(size)], axis=0)
                for right, out in pairs:
                    whole = dot(rows, right, ((1,), (0,)))
                    for n in range(size):
                        piece = whole[n * BLOCK : (n + 1) * BLOCK]
                        if n >= size - step:
                            piece = piece * kept(places[n]).astype(F32)
                        out[blocks(places[n]), :] = piece.astype(BF16)
                    for n in range(size, length):
                        out[blocks(places[n]), :] = jnp.zeros((BLOCK, BLOCK), BF16)

    def inward(k):
        b = lax.rem(k, 2)
        load_fin(k).wait()

        @pl.when(k >= 2)
        def _():
            for copy in saves(k - 2):
                copy.wait()

        products(
            0, k, pieces, xt, ((fin[k, 0], gate_o.at[b]), (fin[k, 1], up_o.at[b])),
            lambda i: keep_in[k, i],
        )
        for copy in saves(k):
            copy.start()

    def outward(i):
        b = lax.rem(i, 2)
        load_dy(i).wait()

        @pl.when(i >= 2)
        def _():
            save_down(i - 2).wait()

        products(1, i, units, ht, ((dy[i], down_o.at[b]),), lambda k: keep_out[k, i])
        save_down(i).start()

    load_xt.wait()

    @pl.loop(0, max(units, pieces))
    def _(n):
        @pl.when(n < units)
        def _():
            inward(n)

        @pl.when(n == 0)
        def _():
            load_ht.wait()

        @pl.when(n < pieces)
        def _():
            outward(n)

    for k in range(max(0, units - 2), units):
        for copy in saves(k):
            copy.wait()
    for i in range(max(0, pieces - 2), pieces):
        save_down(i).wait()


def weight_grads(xt, dy, fin, ht, mask_in, mask_out):
    width, total = xt.shape
    hidden = ht.shape[0]
    pieces, units = width // BLOCK, hidden // BLOCK
    struct = jax.ShapeDtypeStruct
    anywhere = pl.BlockSpec(memory_space=pl.ANY)
    dma = pltpu.SemaphoreType.DMA
    return pl.pallas_call(
        wgrad_kernel,
        out_shape=(
            struct((width, hidden), BF16),
            struct((width, hidden), BF16),
            struct((hidden, width), BF16),
        ),
        in_specs=[anywhere] * 6,
        out_specs=(anywhere,) * 3,
        scratch_shapes=[
            pltpu.VMEM((width, total), BF16),
            pltpu.VMEM((hidden, total), BF16),
            pltpu.VMEM((units, 2, total, BLOCK), BF16),
            pltpu.VMEM((pieces, total, BLOCK), BF16),
            pltpu.VMEM((2, width, BLOCK), BF16),
            pltpu.VMEM((2, width, BLOCK), BF16),
            pltpu.VMEM((2, hidden, BLOCK), BF16),
            pltpu.SMEM((2, max(units, pieces), max(units, pieces) + 1), jnp.int32),
            pltpu.SMEM((units, pieces), jnp.int32),
            pltpu.SMEM((units, pieces), jnp.int32),
            dma((2,)),
            dma, dma, dma((units,)), dma((pieces,)), dma((2,)), dma((2,)), dma((2,)),
        ],
        compiler_params=pltpu.CompilerParams(vmem_limit_bytes=60 * 1024 * 1024),
        cost_estimate=pl.CostEstimate(
            flops=6 * total * width * hidden,
            bytes_accessed=6 * width * hidden + 10 * total * width,
            transcendentals=0,
        ),
        name="wgrad",
    )(xt, dy, fin, ht, mask_in, mask_out)


def local(rows, cols, tokens, w_gate, w_up, w_down, mask_in, mask_out, out_grad):
    share, width = tokens.shape
    hidden = w_gate.shape[1]
    units = hidden // BLOCK
    total = share * cols
    chips = cols // CORES
    chunk = CORES * share
    count = chips * units
    anywhere = pl.BlockSpec(memory_space=pl.ANY)
    dma = pltpu.SemaphoreType.DMA
    struct = jax.ShapeDtypeStruct
    base, tail, xt, dy, fin, ht = pl.pallas_call(
        functools.partial(step_kernel, rows, cols, units),
        out_shape=(
            struct((2, share, width), F32),
            struct((2, share, width), BF16),
            struct((width, total) if turned(chunk) else (total, width), BF16),
            struct((total, width), BF16),
            struct((2, total, hidden), BF16),
            struct((hidden, total) if turned(chunk) else (total, hidden), BF16),
        ),
        in_specs=[anywhere] * 7,
        out_specs=(anywhere,) * 6,
        scratch_shapes=[
            pltpu.VMEM((chips, chunk, width), BF16),
            pltpu.VMEM((chips, chunk, width), BF16),
            pltpu.VMEM((2, width, chunk), BF16),
            pltpu.VMEM((count, 3, chunk, BLOCK), BF16),
            pltpu.VMEM((count, 3, chunk // 2, BLOCK), BF16),
            pltpu.VMEM((count, 3, chunk, BLOCK), BF16),
            pltpu.VMEM((count, BLOCK, chunk) if turned(chunk) else (1, 16, 128), BF16),
            pltpu.VMEM((OWN_SLOTS, 3, chunk, BLOCK), F32),
            pltpu.VMEM((units, 2, width, BLOCK), BF16),
            pltpu.VMEM((units, BLOCK, width), BF16),
            pltpu.VMEM((2, 2, chunk, width), F32),
            pltpu.VMEM((chips, 2, share, width), F32),
            pltpu.VMEM((chips - 1, 2, share, width), BF16),
            pltpu.VMEM((chips - 2, 2, share, width), BF16),
            pltpu.SMEM((units, width // BLOCK), jnp.int32),
            pltpu.SMEM((units, width // BLOCK), jnp.int32),
            dma((2,)),
            dma((2,)), dma((2,)), dma((2,)),
            dma((2, chips - 1)), dma((2, chips - 1)),
            dma((2, chips - 1)), dma((2, chips - 1)),
            dma((units, 3)),
            dma((count, 2, SPLIT)), dma((count, 2, SPLIT)), dma((count, SPLIT)),
            dma((count, SPLIT)), dma((count, 2, SPLIT)), dma((count, 2, SPLIT)),
            dma((chips,)), dma((chips,)), dma((count,)), dma((count,)),
            dma((chips, 2)), dma((chips, 2)),
            dma((chips - 2,)), dma((chips - 2,)),
            dma((2,)),
        ],
        compiler_params=pltpu.CompilerParams(
            collective_id=0, has_side_effects=True, vmem_limit_bytes=63 * 1024 * 1024
        ),
        cost_estimate=pl.CostEstimate(
            flops=12 * total * width * hidden,
            bytes_accessed=6 * width * hidden,
            transcendentals=total * hidden,
        ),
        name="step",
    )(tokens, out_grad, w_gate, w_up, w_down, mask_in, mask_out)
    if not turned(chunk):
        xt, ht = xt.T, ht.T
    nearest = [(i, (i // CORES ^ 1) * CORES + i % CORES) for i in range(cols)]
    moved = lax.ppermute(tail, "col", nearest)
    gate_wgrad, up_wgrad, down_wgrad = weight_grads(xt, dy, fin, ht, mask_in, mask_out)
    output, tokens_grad = [(base[a] + moved[a].astype(F32)).astype(BF16) for a in range(2)]
    return output, tokens_grad, gate_wgrad, up_wgrad, down_wgrad


def solution(mesh):
    placed = (
        P("col", "row"),
        P("row", "col"),
        P("row", "col"),
        P("col", "row"),
        P("col", "row"),
        P("col", "row"),
        P("col", "row"),
    )
    return jax.shard_map(
        functools.partial(local, mesh.shape["row"], mesh.shape["col"]),
        mesh=mesh,
        in_specs=placed,
        out_specs=(
            P("col", "row"),
            P("col", "row"),
            P("row", "col"),
            P("row", "col"),
            P("col", "row"),
        ),
        check_vma=False,
    )
```

```python
import functools

import jax
import jax.numpy as jnp
from jax import lax
from jax.experimental import pallas as pl
from jax.experimental.pallas import tpu as pltpu
from jax.sharding import PartitionSpec as P

BLOCK = 256
CORES = 2
LAG_OWN = 1
LAG_FWD = 2
LAG_USE = 5
OWN_SLOTS = LAG_OWN + 1
KEPT = 10
SAVED = 3
SPLIT = 1
MESH = pl.DeviceIdType.MESH
F32 = jnp.float32
BF16 = jnp.bfloat16


def dot(left, right, dims):
    return lax.dot_general(left, right, (dims, ((), ())), preferred_element_type=F32)


def turned(chunk):
    return chunk % 128 == 0


def flip(chip, j, chips):
    other, bit = chip, 1
    while bit < chips:
        other = other + lax.rem(lax.div(j, bit), 2) * (bit - 2 * bit * lax.rem(lax.div(chip, bit), 2))
        bit *= 2
    return other


def place(q, chips):
    return jnp.where(q == 0, 0, jnp.where(q == chips - 1, 1, q + 1))


def step_kernel(
    rows, cols, units,
    tok, cot, w_gate, w_up, w_down, mask_in, mask_out,
    base, tail, xt_out, dy_out, fin_out, ht_out,
    x, dy, xt, part, other, fin, ht, own, w_in, w_dn, acc, sib, rs_send, rs_recv,
    keep_in, keep_out, keep_s,
    own_s, sib_ss, sib_rs, ag_ss, ag_rs, fw_ss, fw_rs, w_s, p_ss, a_rs, b_rs, fi_ss, fo_ss, f_rs,
    xt_s, dy_s, fin_s, ht_s, rx_ss, rx_rs, rs_ss, rs_rs, end_s,
):
    r = lax.axis_index("row")
    c = lax.axis_index("col")
    chips = cols // CORES
    chip, core = lax.div(c, CORES), lax.rem(c, CORES)
    low = r < rows // 2
    inner = jnp.where(low, r + 1, r - 1)
    outer = jnp.where(low, r - 1, r + 1)
    has_outer = (r > 0) & (r < rows - 1)
    middle = (r == rows // 2 - 1) | (r == rows // 2)
    outermost = jnp.logical_not(has_outer | middle)
    owned = jnp.where(low, 0, 1)
    given = 1 - owned
    share, width = tok.shape
    chunk = CORES * share
    half = chunk // 2
    split = SPLIT
    part_rows = half // split
    pieces = width // BLOCK
    count = chips * units
    last = chips - 1
    turn = turned(chunk)
    sibling = (r, chip * CORES + (1 - core))

    def partner(q):
        return (r, flip(chip, place(q, chips), chips) * CORES + core)

    def rows_of(h, u):
        return pl.ds(pl.multiple_of(h * half + u * part_rows, part_rows), part_rows)

    def shares(e):
        return pl.ds(pl.multiple_of(e * share, share), share)

    def blocks(i):
        return pl.ds(pl.multiple_of(i * BLOCK, BLOCK), BLOCK)

    def chunks(q):
        return pl.ds(pl.multiple_of(q * chunk, chunk), chunk)

    def weights(k):
        return (
            pltpu.make_async_copy(w_gate.at[:, blocks(k)], w_in.at[k, 0], w_s.at[k, 0]),
            pltpu.make_async_copy(w_up.at[:, blocks(k)], w_in.at[k, 1], w_s.at[k, 1]),
            pltpu.make_async_copy(w_down.at[blocks(k), :], w_dn.at[k], w_s.at[k, 2]),
        )

    def own_copy(a):
        src, dst = ((tok, x), (cot, dy))[a]
        return pltpu.make_async_copy(src, dst.at[0, shares(core), :], own_s.at[a])

    masks = [
        pltpu.make_async_copy(mask_in, keep_in, keep_s.at[0]),
        pltpu.make_async_copy(mask_out, keep_out, keep_s.at[1]),
    ]
    for copy in masks:
        copy.start()
    for copy in weights(0):
        copy.start()
    for a in range(2):
        own_copy(a).start()

    barrier = pltpu.get_barrier_semaphore()
    pl.semaphore_signal(barrier, inc=1, device_id=(inner, c), device_id_type=MESH)
    pl.semaphore_signal(barrier, inc=1, device_id=sibling, device_id_type=MESH)
    for q in range(1, chips):
        pl.semaphore_signal(barrier, inc=1, device_id=partner(q), device_id_type=MESH)

    @pl.when(has_outer)
    def _():
        pl.semaphore_signal(barrier, inc=1, device_id=(outer, c), device_id_type=MESH)

    def prepare(k):
        for copy in weights(k):
            copy.wait()

        @pl.loop(0, pieces)
        def _(i):
            at = blocks(i)
            keep = keep_in[k, i].astype(F32)
            w_in[k, 0, at, :] = (w_in[k, 0, at, :].astype(F32) * keep).astype(BF16)
            w_in[k, 1, at, :] = (w_in[k, 1, at, :].astype(F32) * keep).astype(BF16)
            w_dn[k, :, at] = (w_dn[k, :, at].astype(F32) * keep_out[k, i].astype(F32)).astype(BF16)

    for copy in masks:
        copy.wait()
    prepare(0)

    def first_half(e, arrays):
        at = shares(e)
        for j in arrays:
            if j < 2:
                own[0, j, at, :] = dot(x[0, at, :], w_in[0, j], ((1,), (0,)))
            else:
                own[0, j, at, :] = dot(dy[0, at, :], w_dn[0], ((1,), (1,)))

    for a in range(2):
        own_copy(a).wait()
    first_half(core, (0, 1, 2))
    pl.semaphore_wait(barrier, jnp.where(has_outer, chips + 2, chips + 1))

    def to_sibling(a):
        src, dst = ((tok, x), (cot, dy))[a]
        return pltpu.make_async_remote_copy(
            src_ref=src, dst_ref=dst.at[0, shares(core), :], send_sem=sib_ss.at[a],
            recv_sem=sib_rs.at[a], device_id=sibling, device_id_type=MESH,
        )

    def to_chip(a, q):
        src, dst = ((tok, x), (cot, dy))[a]
        return pltpu.make_async_remote_copy(
            src_ref=src, dst_ref=dst.at[q, shares(core), :], send_sem=ag_ss.at[a, q - 1],
            recv_sem=ag_rs.at[a, q - 1], device_id=partner(q), device_id_type=MESH,
        )

    def forward(a, q):
        ref = (x, dy)[a].at[q, shares(core), :]
        return pltpu.make_async_remote_copy(
            src_ref=ref, dst_ref=ref, send_sem=fw_ss.at[a, q - 1],
            recv_sem=fw_rs.at[a, q - 1], device_id=sibling, device_id_type=MESH,
        )

    for a in range(2):
        to_sibling(a).start()
    if units > 1:
        for copy in weights(1):
            copy.start()

    def send_inner(t, h, u):
        ref = part.at[t, :, rows_of(h, u), :]
        return pltpu.make_async_remote_copy(
            src_ref=ref, dst_ref=ref, send_sem=p_ss.at[t, h, u],
            recv_sem=a_rs.at[t, h, u], device_id=(inner, c), device_id_type=MESH,
        )

    def send_middle(t, u):
        return pltpu.make_async_remote_copy(
            src_ref=part.at[t, :, rows_of(given, u), :], dst_ref=other.at[t, :, rows_of(0, u), :],
            send_sem=p_ss.at[t, given, u], recv_sem=b_rs.at[t, u], device_id=(inner, c), device_id_type=MESH,
        )

    def share_inner(t, h, u):
        ref = fin.at[t, :, rows_of(h, u), :]
        return pltpu.make_async_remote_copy(
            src_ref=ref, dst_ref=ref, send_sem=fi_ss.at[t, u],
            recv_sem=f_rs.at[t, h, u], device_id=(inner, c), device_id_type=MESH,
        )

    def share_outer(t, h, u):
        ref = fin.at[t, :, rows_of(h, u), :]
        return pltpu.make_async_remote_copy(
            src_ref=ref, dst_ref=ref, send_sem=fo_ss.at[t, h, u],
            recv_sem=f_rs.at[t, h, u], device_id=(outer, c), device_id_type=MESH,
        )

    def save_xt(q):
        if not turn:
            return pltpu.make_async_copy(x.at[q], xt_out.at[chunks(q), :], xt_s.at[q])
        return pltpu.make_async_copy(xt.at[lax.rem(q, 2)], xt_out.at[:, chunks(q)], xt_s.at[q])

    def save_dy(q):
        return pltpu.make_async_copy(dy.at[q], dy_out.at[chunks(q), :], dy_s.at[q])

    def save_fin(t):
        q, k = lax.div(t, units), lax.rem(t, units)
        return pltpu.make_async_copy(
            fin.at[t, pl.ds(0, 2)], fin_out.at[:, chunks(q), blocks(k)], fin_s.at[t]
        )

    def save_ht(t):
        q, k = lax.div(t, units), lax.rem(t, units)
        if not turn:
            return pltpu.make_async_copy(fin.at[t, 2], ht_out.at[chunks(q), blocks(k)], ht_s.at[t])
        return pltpu.make_async_copy(ht.at[t], ht_out.at[blocks(k), chunks(q)], ht_s.at[t])

    def produce(t):
        q, k = lax.div(t, units), lax.rem(t, units)
        s = lax.rem(t, OWN_SLOTS)

        @pl.when((k == 0) & (q > 0))
        def _():
            for a in range(2):
                forward(a, q).wait_recv()

        @pl.when(t + 2 < units)
        def _():
            for copy in weights(t + 2):
                copy.start()

        @pl.when((q == 0) & (k > 0))
        def _():
            prepare(k)

        @pl.when(t == 0)
        def _():
            to_sibling(0).wait_recv()
            first_half(1 - core, (0, 1))
            to_sibling(1).wait_recv()
            first_half(1 - core, (2,))

        @pl.when(t > 0)
        def _():
            own[s, 0] = dot(x[q], w_in[k, 0], ((1,), (0,)))
            own[s, 1] = dot(x[q], w_in[k, 1], ((1,), (0,)))
            own[s, 2] = dot(dy[q], w_dn[k], ((1,), (1,)))

    def reduce(t):
        s = lax.rem(t, OWN_SLOTS)

        def rounded(h, u):
            at = rows_of(h, u)

            @pl.when(has_outer)
            def _():
                send_inner(t, h, u).wait_recv()
                for j in range(3):
                    part[t, j, at, :] = (own[s, j, at, :] + part[t, j, at, :].astype(F32)).astype(BF16)

            @pl.when(jnp.logical_not(has_outer))
            def _():
                for j in range(3):
                    part[t, j, at, :] = own[s, j, at, :].astype(BF16)

        @pl.loop(0, split)
        def _(u):
            rounded(given, u)

            @pl.when(middle)
            def _():
                send_middle(t, u).start()

            @pl.when(jnp.logical_not(middle))
            def _():
                send_inner(t, given, u).start()

        @pl.when(jnp.logical_not(middle))
        def _():
            @pl.loop(0, split)
            def _(u):
                rounded(owned, u)
                send_inner(t, owned, u).start()

    def reduce_first():
        @pl.when(outermost)
        def _():
            at = shares(1 - core)
            for j in range(3):
                part[0, j, at, :] = own[0, j, at, :].astype(BF16)
            send_inner(0, 1 - core, 0).start()

        @pl.when(jnp.logical_not(outermost))
        def _():
            reduce(0)

    def send_first():
        at = shares(core)
        for j in range(3):
            part[0, j, at, :] = own[0, j, at, :].astype(BF16)
        send_inner(0, core, 0).start()

    def finish(t):
        s = lax.rem(t, OWN_SLOTS)

        def one(u):
            at = rows_of(owned, u)
            there = rows_of(0, u)

            @pl.when(has_outer)
            def _():
                send_inner(t, owned, u).wait_recv()
                for j in range(3):
                    own[s, j, at, :] += part[t, j, at, :].astype(F32)

            send_middle(t, u).wait_recv()
            gate = own[s, 0, at, :] + other[t, 0, there, :].astype(F32)
            up = own[s, 1, at, :] + other[t, 1, there, :].astype(F32)
            grad = own[s, 2, at, :] + other[t, 2, there, :].astype(F32)
            sig = jax.nn.sigmoid(gate)
            act = gate * sig
            fin[t, 0, at, :] = (grad * up * sig * (1.0 + gate * (1.0 - sig))).astype(BF16)
            fin[t, 1, at, :] = (grad * act).astype(BF16)
            fin[t, 2, at, :] = (act * up).astype(BF16)

            share_inner(t, owned, u).start()

            @pl.when(has_outer)
            def _():
                share_outer(t, owned, u).start()

        @pl.when(middle)
        def _():
            pl.loop(0, split)(one)

    def arrived(t):
        def one(h, u):
            share_inner(t, h, u).wait_recv()

            @pl.when(has_outer)
            def _():
                share_outer(t, h, u).start()

        @pl.loop(0, split)
        def _(u):
            one(given, u)

            @pl.when(jnp.logical_not(middle))
            def _():
                one(owned, u)

    def transpose_tokens(t):
        q, k = lax.div(t, units), lax.rem(t, units)

        if turn:
            @pl.when((k == 0) & (q >= 2))
            def _():
                save_xt(q - 2).wait()

            @pl.loop(lax.div(k * pieces, units), lax.div((k + 1) * pieces, units))
            def _(i):
                xt[lax.rem(q, 2), blocks(i), :] = x[q, :, blocks(i)].T

        @pl.when(k == units - 1)
        def _():
            save_xt(q).start()
            save_dy(q).start()

        @pl.when((k == max(0, units - 2)) & (q + 1 < chips))
        def _():
            for a in range(2):
                to_chip(a, q + 1).wait_recv()
                forward(a, q + 1).start()

    def to_sibling_sum(q, a):
        return pltpu.make_async_remote_copy(
            src_ref=acc.at[lax.rem(q, 2), a, shares(1 - core), :], dst_ref=sib.at[q, a],
            send_sem=rx_ss.at[q, a], recv_sem=rx_rs.at[q, a], device_id=sibling, device_id_type=MESH,
        )

    def scatter(q):
        return pltpu.make_async_remote_copy(
            src_ref=rs_send.at[q - 1], dst_ref=rs_recv.at[q - 1], send_sem=rs_ss.at[q - 1],
            recv_sem=rs_rs.at[q - 1], device_id=partner(q), device_id_type=MESH,
        )

    def consume(t):
        q, k = lax.div(t, units), lax.rem(t, units)
        b = lax.rem(q, 2)

        @pl.when(k == 0)
        def _():
            acc[b] = jnp.zeros_like(acc[b])

        save_fin(t).start()
        acc[b, 0] += dot(fin[t, 2], w_dn[k], ((1,), (0,)))

        @pl.when(k == units - 1)
        def _():
            to_sibling_sum(q, 0).start()

        acc[b, 1] += dot(fin[t, 0], w_in[k, 0], ((1,), (1,))) + dot(
            fin[t, 1], w_in[k, 1], ((1,), (1,))
        )

        @pl.when(k == units - 1)
        def _():
            to_sibling_sum(q, 1).start()

        if turn:
            ht[t] = fin[t, 2].T
        save_ht(t).start()

    def sent(t):
        @pl.loop(0, split)
        def _(u):
            @pl.when(middle)
            def _():
                send_middle(t, u).wait_send()
                share_inner(t, owned, u).wait_send()

            @pl.when(jnp.logical_not(middle))
            def _():
                for h in range(2):
                    send_inner(t, h, u).wait_send()

            @pl.when(has_outer)
            def _():
                for h in range(2):
                    share_outer(t, h, u).wait_send()

    def saved(t):
        save_fin(t).wait()
        save_ht(t).wait()

    def gathered():
        for a in range(2):
            to_sibling(a).wait_send()
            for q in range(1, chips):
                to_chip(a, q).wait_send()
                forward(a, q).wait_send()
        for q in range(last):
            save_dy(q).wait()
            if q < last - 1 and turn:
                continue
            save_xt(q).wait()

    def settle(q):
        at = shares(core)
        for a in range(2):
            to_sibling_sum(q, a).wait()
            sib[q, a] += acc[lax.rem(q, 2), a, at, :]

    @pl.when(outermost)
    def _():
        send_first()

    @pl.loop(0, count + LAG_USE)
    def _(t):
        @pl.when(t < count)
        def _():
            produce(t)

            @pl.when(t == 0)
            def _():
                reduce_first()

            @pl.when(t > 0)
            def _():
                reduce(t)

        @pl.when(t == 0)
        def _():
            for q in range(1, chips):
                for a in range(2):
                    to_chip(a, q).start()

        @pl.when((t >= LAG_OWN) & (t < count + LAG_OWN))
        def _():
            finish(t - LAG_OWN)

        @pl.when(has_outer & (t >= LAG_FWD) & (t < count + LAG_FWD))
        def _():
            arrived(t - LAG_FWD)

        @pl.when((t >= KEPT) & (t < count + KEPT))
        def _():
            sent(t - KEPT)

        @pl.when(t == count - 1)
        def _():
            gathered()

        @pl.when(t >= LAG_USE)
        def _():
            u = t - LAG_USE

            @pl.when(jnp.logical_not(has_outer))
            def _():
                arrived(u)

            consume(u)

            @pl.when(u >= SAVED)
            def _():
                saved(u - SAVED)

            q = lax.div(u, units) - 1

            @pl.when((lax.rem(u, units) == 1) & (q >= 0))
            def _():
                settle(q)

                @pl.when(q > 0)
                def _():
                    for a in range(2):
                        rs_send[q - 1, a] = sib[q, a].astype(BF16)
                    scatter(q).start()

        @pl.when(t < count)
        def _():
            transpose_tokens(t)

    for q in range(1, last):
        scatter(q).wait()
        for a in range(2):
            sib[0, a] += rs_recv[q - 1, a].astype(F32)
    save_base = pltpu.make_async_copy(sib.at[0], base, end_s.at[0])
    save_base.start()
    for a in range(2):
        to_sibling_sum(last, a).wait()
        rs_send[last - 1, a] = (sib[last, a] + acc[last % 2, a, shares(core), :]).astype(BF16)
    save_tail = pltpu.make_async_copy(rs_send.at[last - 1], tail, end_s.at[1])
    save_tail.start()

    @pl.loop(max(0, count - SAVED), count)
    def _(t):
        saved(t)

    @pl.loop(max(0, count + LAG_USE - KEPT), count)
    def _(t):
        sent(t)

    save_dy(last).wait()
    save_xt(last).wait()
    save_base.wait()
    save_tail.wait()


def wgrad_kernel(
    xt_in, dy_in, fin_in, ht_in, mask_in, mask_out, gate_w, up_w, down_w,
    xt, ht, fin, dy, gate_o, up_o, down_o, order, keep_in, keep_out, keep_s, xt_s, ht_s, fin_s, dy_s, gate_s, up_s, down_s,
):
    pieces = xt.shape[0] // BLOCK
    units = ht.shape[0] // BLOCK

    def blocks(i):
        return pl.ds(pl.multiple_of(i * BLOCK, BLOCK), BLOCK)

    def load_fin(k):
        return pltpu.make_async_copy(fin_in.at[:, :, blocks(k)], fin.at[k], fin_s.at[k])

    def load_dy(i):
        return pltpu.make_async_copy(dy_in.at[:, blocks(i)], dy.at[i], dy_s.at[i])

    def saves(k):
        b = lax.rem(k, 2)
        return (
            pltpu.make_async_copy(gate_o.at[b], gate_w.at[:, blocks(k)], gate_s.at[b]),
            pltpu.make_async_copy(up_o.at[b], up_w.at[:, blocks(k)], up_s.at[b]),
        )

    def save_down(i):
        b = lax.rem(i, 2)
        return pltpu.make_async_copy(down_o.at[b], down_w.at[:, blocks(i)], down_s.at[b])

    masks = [
        pltpu.make_async_copy(mask_in, keep_in, keep_s.at[0]),
        pltpu.make_async_copy(mask_out, keep_out, keep_s.at[1]),
    ]
    load_xt = pltpu.make_async_copy(xt_in, xt, xt_s)
    load_ht = pltpu.make_async_copy(ht_in, ht, ht_s)
    load_fin(0).start()
    load_xt.start()
    for copy in masks:
        copy.start()
    load_dy(0).start()
    load_ht.start()

    @pl.loop(1, units)
    def _(k):
        load_fin(k).start()

    @pl.loop(1, pieces)
    def _(i):
        load_dy(i).start()

    def sort(kind, column, length, kept):
        def put(i, n):
            keep = kept(i)
            order[kind, column, jnp.where(keep != 0, n, length - 1 - (i - n))] = i
            return n + keep

        order[kind, column, length] = lax.fori_loop(0, length, put, 0)

    for copy in masks:
        copy.wait()

    @pl.loop(0, units)
    def _(k):
        sort(0, k, pieces, lambda i: keep_in[k, i])

    @pl.loop(0, pieces)
    def _(i):
        sort(1, i, units, lambda k: keep_out[k, i])

    def products(kind, column, length, left, pairs, kept):
        kept_count = order[kind, column, length]
        step = max(1, length // 8)
        for size in range(step, length + 1, step):
            lowest = kept_count > size - step if size > step else kept_count >= 0

            @pl.when(lowest & (kept_count <= size))
            def _():
                places = [order[kind, column, n] for n in range(length)]
                rows = jnp.concatenate([left[blocks(places[n]), :] for n in range(size)], axis=0)
                for right, out in pairs:
                    whole = dot(rows, right, ((1,), (0,)))
                    for n in range(size):
                        piece = whole[n * BLOCK : (n + 1) * BLOCK]
                        if n >= size - step:
                            piece = piece * kept(places[n]).astype(F32)
                        out[blocks(places[n]), :] = piece.astype(BF16)
                    for n in range(size, length):
                        out[blocks(places[n]), :] = jnp.zeros((BLOCK, BLOCK), BF16)

    def inward(k):
        b = lax.rem(k, 2)
        load_fin(k).wait()

        @pl.when(k >= 2)
        def _():
            for copy in saves(k - 2):
                copy.wait()

        products(
            0, k, pieces, xt, ((fin[k, 0], gate_o.at[b]), (fin[k, 1], up_o.at[b])),
            lambda i: keep_in[k, i],
        )
        for copy in saves(k):
            copy.start()

    def outward(i):
        b = lax.rem(i, 2)
        load_dy(i).wait()

        @pl.when(i >= 2)
        def _():
            save_down(i - 2).wait()

        products(1, i, units, ht, ((dy[i], down_o.at[b]),), lambda k: keep_out[k, i])
        save_down(i).start()

    load_xt.wait()

    @pl.loop(0, max(units, pieces))
    def _(n):
        @pl.when(n < units)
        def _():
            inward(n)

        @pl.when(n == 0)
        def _():
            load_ht.wait()

        @pl.when(n < pieces)
        def _():
            outward(n)

    for k in range(max(0, units - 2), units):
        for copy in saves(k):
            copy.wait()
    for i in range(max(0, pieces - 2), pieces):
        save_down(i).wait()


def weight_grads(xt, dy, fin, ht, mask_in, mask_out):
    width, total = xt.shape
    hidden = ht.shape[0]
    pieces, units = width // BLOCK, hidden // BLOCK
    struct = jax.ShapeDtypeStruct
    anywhere = pl.BlockSpec(memory_space=pl.ANY)
    dma = pltpu.SemaphoreType.DMA
    return pl.pallas_call(
        wgrad_kernel,
        out_shape=(
            struct((width, hidden), BF16),
            struct((width, hidden), BF16),
            struct((hidden, width), BF16),
        ),
        in_specs=[anywhere] * 6,
        out_specs=(anywhere,) * 3,
        scratch_shapes=[
            pltpu.VMEM((width, total), BF16),
            pltpu.VMEM((hidden, total), BF16),
            pltpu.VMEM((units, 2, total, BLOCK), BF16),
            pltpu.VMEM((pieces, total, BLOCK), BF16),
            pltpu.VMEM((2, width, BLOCK), BF16),
            pltpu.VMEM((2, width, BLOCK), BF16),
            pltpu.VMEM((2, hidden, BLOCK), BF16),
            pltpu.SMEM((2, max(units, pieces), max(units, pieces) + 1), jnp.int32),
            pltpu.SMEM((units, pieces), jnp.int32),
            pltpu.SMEM((units, pieces), jnp.int32),
            dma((2,)),
            dma, dma, dma((units,)), dma((pieces,)), dma((2,)), dma((2,)), dma((2,)),
        ],
        compiler_params=pltpu.CompilerParams(vmem_limit_bytes=60 * 1024 * 1024),
        cost_estimate=pl.CostEstimate(
            flops=6 * total * width * hidden,
            bytes_accessed=6 * width * hidden + 10 * total * width,
            transcendentals=0,
        ),
        name="wgrad",
    )(xt, dy, fin, ht, mask_in, mask_out)


def local(rows, cols, tokens, w_gate, w_up, w_down, mask_in, mask_out, out_grad):
    share, width = tokens.shape
    hidden = w_gate.shape[1]
    units = hidden // BLOCK
    total = share * cols
    chips = cols // CORES
    chunk = CORES * share
    count = chips * units
    anywhere = pl.BlockSpec(memory_space=pl.ANY)
    dma = pltpu.SemaphoreType.DMA
    struct = jax.ShapeDtypeStruct
    base, tail, xt, dy, fin, ht = pl.pallas_call(
        functools.partial(step_kernel, rows, cols, units),
        out_shape=(
            struct((2, share, width), F32),
            struct((2, share, width), BF16),
            struct((width, total) if turned(chunk) else (total, width), BF16),
            struct((total, width), BF16),
            struct((2, total, hidden), BF16),
            struct((hidden, total) if turned(chunk) else (total, hidden), BF16),
        ),
        in_specs=[anywhere] * 7,
        out_specs=(anywhere,) * 6,
        scratch_shapes=[
            pltpu.VMEM((chips, chunk, width), BF16),
            pltpu.VMEM((chips, chunk, width), BF16),
            pltpu.VMEM((2, width, chunk), BF16),
            pltpu.VMEM((count, 3, chunk, BLOCK), BF16),
            pltpu.VMEM((count, 3, chunk // 2, BLOCK), BF16),
            pltpu.VMEM((count, 3, chunk, BLOCK), BF16),
            pltpu.VMEM((count, BLOCK, chunk) if turned(chunk) else (1, 16, 128), BF16),
            pltpu.VMEM((OWN_SLOTS, 3, chunk, BLOCK), F32),
            pltpu.VMEM((units, 2, width, BLOCK), BF16),
            pltpu.VMEM((units, BLOCK, width), BF16),
            pltpu.VMEM((2, 2, chunk, width), F32),
            pltpu.VMEM((chips, 2, share, width), F32),
            pltpu.VMEM((chips - 1, 2, share, width), BF16),
            pltpu.VMEM((chips - 2, 2, share, width), BF16),
            pltpu.SMEM((units, width // BLOCK), jnp.int32),
            pltpu.SMEM((units, width // BLOCK), jnp.int32),
            dma((2,)),
            dma((2,)), dma((2,)), dma((2,)),
            dma((2, chips - 1)), dma((2, chips - 1)),
            dma((2, chips - 1)), dma((2, chips - 1)),
            dma((units, 3)),
            dma((count, 2, SPLIT)), dma((count, 2, SPLIT)), dma((count, SPLIT)),
            dma((count, SPLIT)), dma((count, 2, SPLIT)), dma((count, 2, SPLIT)),
            dma((chips,)), dma((chips,)), dma((count,)), dma((count,)),
            dma((chips, 2)), dma((chips, 2)),
            dma((chips - 2,)), dma((chips - 2,)),
            dma((2,)),
        ],
        compiler_params=pltpu.CompilerParams(
            collective_id=0, has_side_effects=True, vmem_limit_bytes=63 * 1024 * 1024
        ),
        cost_estimate=pl.CostEstimate(
            flops=12 * total * width * hidden,
            bytes_accessed=6 * width * hidden,
            transcendentals=total * hidden,
        ),
        name="step",
    )(tokens, out_grad, w_gate, w_up, w_down, mask_in, mask_out)
    if not turned(chunk):
        xt, ht = xt.T, ht.T
    nearest = [(i, (i // CORES ^ 1) * CORES + i % CORES) for i in range(cols)]
    moved = lax.ppermute(tail, "col", nearest)
    gate_wgrad, up_wgrad, down_wgrad = weight_grads(xt, dy, fin, ht, mask_in, mask_out)
    output, tokens_grad = [(base[a] + moved[a].astype(F32)).astype(BF16) for a in range(2)]
    return output, tokens_grad, gate_wgrad, up_wgrad, down_wgrad


def solution(mesh):
    placed = (
        P("col", "row"),
        P("row", "col"),
        P("row", "col"),
        P("col", "row"),
        P("col", "row"),
        P("col", "row"),
        P("col", "row"),
    )
    return jax.shard_map(
        functools.partial(local, mesh.shape["row"], mesh.shape["col"]),
        mesh=mesh,
        in_specs=placed,
        out_specs=(
            P("col", "row"),
            P("col", "row"),
            P("row", "col"),
            P("row", "col"),
            P("col", "row"),
        ),
        check_vma=False,
    )
```
